128 devices in a mesh: blk: 4 (over x_lo, core), inner: 32 (over y, x_hi, z).
Axes of the slice: x: 4 (x_hi: 2, x_lo: 2; x = x_hi * 2 + x_lo), y: 4, z: 4, core: 2. Of those that a mesh axis runs over, the one named last changes fastest.
Arguments:
- queries: bfloat16 [32768, 4096], P(('blk', 'inner')), may hold values from -5 to 5
- keys: bfloat16 [32768, 512], P(('blk', 'inner')), may hold values from -5 to 5
- values: bfloat16 [32768, 512], P(('blk', 'inner')), may hold values from -6 to 6
- out_grad: bfloat16 [32768, 4096], P(('blk', 'inner')), may hold values from -6 to 6
- doc_lengths: int32 [64], replicated, may hold values from 1 to 768, 32768 in all
Outputs:
- attended: bfloat16 [32768, 4096], P(('blk', 'inner'))
- query_grad: bfloat16 [32768, 4096], P(('blk', 'inner'))
- key_grad: bfloat16 [32768, 512], P(('blk', 'inner'))
- value_grad: bfloat16 [32768, 512], P(('blk', 'inner'))
The draws below stay inside these ranges and needn't reach their ends.
All inputs are finite; a program needn't handle non-finite values.
Results may differ from the reference program's by a relative error of at most 0.025.
Values may be sent and summed in bfloat16 or wider, within the bound.
A program may use at most 128 MiB of HBM per device.

```python
import math
import jax
import jax.numpy as jnp
import numpy as np
from jax import lax

HEAD_SIZE = 128
QUERY_HEADS = 32
KEY_VALUE_HEADS = 4
TOK_DEV = 256
SPAN = 4
PACKED_TOKENS = 32768
MAXDOC = 768
DOCS = 64


def draw_queries(key, part):
    query_group_width = QUERY_HEADS // KEY_VALUE_HEADS
    quad_shape = (PACKED_TOKENS, KEY_VALUE_HEADS, query_group_width, HEAD_SIZE)
    random_base_sample = jnp.clip(jax.random.normal(jax.random.fold_in(key, 1), quad_shape, jnp.float32), -4.0, 4.0)
    return random_base_sample.reshape(PACKED_TOKENS, QUERY_HEADS * HEAD_SIZE).astype(jnp.bfloat16)


def draw_keys(key, part):
    triple_shape = (PACKED_TOKENS, KEY_VALUE_HEADS, HEAD_SIZE)
    random_base_sample = jnp.clip(jax.random.normal(jax.random.fold_in(key, 2), triple_shape, jnp.float32), -4.0, 4.0)
    return random_base_sample.reshape(PACKED_TOKENS, KEY_VALUE_HEADS * HEAD_SIZE).astype(jnp.bfloat16)


def shard_levels(stream_key, extent, split, least, high):
    loudness, own = 1.0, jax.random.fold_in(stream_key, 6)
    for axis_at, parts in split:
        draws = jnp.exp(jax.random.uniform(jax.random.fold_in(own, axis_at), (parts,), jnp.float32, least / len(split), high / len(split)))
        loudness = loudness * jnp.repeat(draws, extent[axis_at] // parts).reshape([-1 if axis == axis_at else 1 for axis in range(len(extent))])
    return loudness


def length_profile(count, total, reach, slope):
    weights = [(1 << 20) // math.isqrt(grade ** slope) + 1 for grade in range(2, count + 1)]
    spare, holding = total - reach - (count - 1), [1] * (count - 1)
    while spare > 0:
        candidates = [i for i in range(count - 1) if holding[i] < reach]
        pool, budget = sum([weights[i] for i in candidates]), spare
        for i in candidates:
            extra = min(reach - holding[i], max(1, budget * weights[i] // pool), spare)
            holding[i] = holding[i] + extra
            spare = spare - extra
    return np.array([reach] + holding)


def uneven(own_key, amount, total, most, slope):
    if amount == 2:
        one = jax.random.randint(own_key, (), max(1, total - most), min(most, total - 1) + 1)
        return jnp.stack([one, total - one])
    lengths = jnp.asarray(length_profile(amount, total, most, slope), jnp.int32)
    pairs = (amount - 1) // 2
    giver, sink = lengths[1:1 + 2 * pairs:2], lengths[2:2 + 2 * pairs:2]
    margin = jnp.minimum(giver - 1, most - sink)
    passed = jax.random.randint(jax.random.fold_in(own_key, 1), (pairs,), 0, 1 << 20) % (margin + 1)
    lengths = lengths.at[1:1 + 2 * pairs:2].set(giver - passed).at[2:2 + 2 * pairs:2].set(sink + passed)
    return lengths[jax.random.permutation(jax.random.fold_in(own_key, 2), amount)]


def bell_draw(rng, shape, width, bound, pieces=(), kind=jnp.bfloat16):
    values = jax.random.normal(rng, shape, jnp.float32) * width
    if len(pieces) > 0:
        values = shard_levels(rng, shape, pieces, -0.22, 0.18) * values
    return jnp.clip(values, min=-bound, max=bound).astype(kind)


def setup_inputs(seed: int = 0) -> dict:
    seeds = jax.random.split(jax.random.key(seed), 6)
    return {
        "queries": draw_queries(jax.random.fold_in(seeds[5], 71), 0),
        "keys": draw_keys(jax.random.fold_in(seeds[5], 71), 0),
        "values": bell_draw(seeds[2], (PACKED_TOKENS, KEY_VALUE_HEADS * HEAD_SIZE), 1.0, 6.0, ((0, 128),)),
        "out_grad": bell_draw(seeds[3], (PACKED_TOKENS, QUERY_HEADS * HEAD_SIZE), 1.0, 6.0, ((0, 128),)),
        "doc_lengths": uneven(seeds[4], DOCS, PACKED_TOKENS, MAXDOC, 2).astype(jnp.int32),
    }


def doc_index(positions, doc_lengths):
    doc_ends = jnp.cumsum(doc_lengths).astype(jnp.int32)
    return lax.optimization_barrier(jnp.sum((doc_ends[None, :] <= positions[:, None]).astype(jnp.int32), axis=1)).astype(jnp.int32)

def block_terms(query_block, key_window_slice, value_window_slice, gradient_block, allowed):
    query_row_list = query_block.shape[0]
    sliding_frame = key_window_slice.shape[0]
    query_group_width = QUERY_HEADS // KEY_VALUE_HEADS
    score_scale = 1.0 / math.sqrt(HEAD_SIZE)
    query_quad = query_block.astype(jnp.float32).reshape(query_row_list, KEY_VALUE_HEADS, query_group_width, HEAD_SIZE)
    gradient_quad = gradient_block.astype(jnp.float32).reshape(query_row_list, KEY_VALUE_HEADS, query_group_width, HEAD_SIZE)
    key_triple = key_window_slice.astype(jnp.float32).reshape(sliding_frame, KEY_VALUE_HEADS, HEAD_SIZE)
    value_triple = value_window_slice.astype(jnp.float32).reshape(sliding_frame, KEY_VALUE_HEADS, HEAD_SIZE)
    scores = jnp.einsum('thgd,whd->hgtw', query_quad, key_triple) * score_scale
    scores = jnp.where(allowed[None, None], scores, -jnp.inf)
    row_max = lax.optimization_barrier(jnp.max(scores, axis=-1, keepdims=True))
    exp_scores = jnp.exp(scores - row_max)
    weights = (exp_scores / lax.optimization_barrier(jnp.sum(exp_scores, axis=-1, keepdims=True))).astype(jnp.bfloat16)
    weights_wide = lax.optimization_barrier(weights).astype(jnp.float32)
    attended = jnp.einsum('hgtw,whd->thgd', weights_wide, value_triple).astype(jnp.bfloat16)
    attended_wide = lax.optimization_barrier(attended).astype(jnp.float32)
    row_delta = jnp.einsum('thgd,thgd->hgt', gradient_quad, attended_wide)
    prob_grad = jnp.einsum('thgd,whd->hgtw', gradient_quad, value_triple)
    score_grad = (weights_wide * (prob_grad - row_delta[..., None]) * score_scale).astype(jnp.bfloat16)
    score_wide = lax.optimization_barrier(score_grad).astype(jnp.float32)
    query_factor = jnp.einsum('hgtw,whd->thgd', score_wide, key_triple).astype(jnp.bfloat16)
    key_portion = jnp.einsum('hgtw,thgd->whd', score_wide, query_quad)
    value_portion = jnp.einsum('hgtw,thgd->whd', weights_wide, gradient_quad)
    return (attended, query_factor, key_portion.reshape(sliding_frame, KEY_VALUE_HEADS * HEAD_SIZE), value_portion.reshape(sliding_frame, KEY_VALUE_HEADS * HEAD_SIZE))

def reference(queries, keys, values, out_grad, doc_lengths):
    blocks = PACKED_TOKENS // TOK_DEV
    backward_row_list = (SPAN - 1) * TOK_DEV
    sliding_frame = SPAN * TOK_DEV
    pad_keys = jnp.concatenate([jnp.zeros((backward_row_list, keys.shape[1]), keys.dtype), keys], axis=0)
    pad_values = jnp.concatenate([jnp.zeros((backward_row_list, values.shape[1]), values.dtype), values], axis=0)

    def scan_step(totals, block_index):
        key_total, value_total = totals
        row_start = (block_index * TOK_DEV).astype(jnp.int32)
        query_block = lax.dynamic_slice_in_dim(queries, row_start, TOK_DEV, 0)
        gradient_block = lax.dynamic_slice_in_dim(out_grad, row_start, TOK_DEV, 0)
        key_window_slice = lax.dynamic_slice_in_dim(pad_keys, row_start, sliding_frame, 0)
        value_window_slice = lax.dynamic_slice_in_dim(pad_values, row_start, sliding_frame, 0)
        query_pos = row_start + jnp.arange(TOK_DEV, dtype=jnp.int32)
        key_pos = row_start - backward_row_list + jnp.arange(sliding_frame, dtype=jnp.int32)
        same_doc = doc_index(key_pos, doc_lengths)[None, :] == doc_index(query_pos, doc_lengths)[:, None]
        allowed = (key_pos[None, :] <= query_pos[:, None]) & (key_pos[None, :] >= 0) & same_doc
        attended, query_factor, key_portion, value_portion = block_terms(query_block, key_window_slice, value_window_slice, gradient_block, allowed)
        previous = lax.dynamic_slice_in_dim(key_total, row_start, sliding_frame, 0)
        key_total = lax.dynamic_update_slice_in_dim(key_total, previous + key_portion, row_start, 0)
        previous = lax.dynamic_slice_in_dim(value_total, row_start, sliding_frame, 0)
        value_total = lax.dynamic_update_slice_in_dim(value_total, previous + value_portion, row_start, 0)
        return ((key_total, value_total), (attended.reshape(TOK_DEV, QUERY_HEADS * HEAD_SIZE), query_factor.reshape(TOK_DEV, QUERY_HEADS * HEAD_SIZE)))
    initial_totals = (jnp.zeros((PACKED_TOKENS + backward_row_list, KEY_VALUE_HEADS * HEAD_SIZE), jnp.float32), jnp.zeros((PACKED_TOKENS + backward_row_list, KEY_VALUE_HEADS * HEAD_SIZE), jnp.float32))
    (key_total, value_total), (attended_all, query_all) = lax.scan(scan_step, initial_totals, jnp.arange(blocks, dtype=jnp.int32))
    return (attended_all.reshape(PACKED_TOKENS, QUERY_HEADS * HEAD_SIZE), query_all.reshape(PACKED_TOKENS, QUERY_HEADS * HEAD_SIZE), key_total[backward_row_list:].astype(jnp.bfloat16), value_total[backward_row_list:].astype(jnp.bfloat16))
```

```python
import math

import jax
import jax.numpy as jnp
from jax import lax
from jax.experimental import pallas as pl
from jax.experimental.pallas import tpu as pltpu
from jax.sharding import PartitionSpec as P

HEAD = 128
KV_HEADS = 4
GROUP = 8
SPAN = 4
SUB = 128
MESH = pl.DeviceIdType.MESH
NT = (((1,), (1,)), ((), ()))
NN = (((1,), (0,)), ((), ()))


def dot(a, b, dims):
    return lax.dot_general(a, b, dims, preferred_element_type=jnp.float32)


def fold_rows(x, op):
    rows = x.shape[0]
    parts = [x[r : r + 8] for r in range(0, rows, 8)]
    while len(parts) > 1:
        parts = [op(parts[i], parts[i + 1]) for i in range(0, len(parts), 2)]
    return parts[0]


def kernel(
    q_hbm,
    k_hbm,
    v_hbm,
    g_hbm,
    len_ref,
    att_ref,
    dq_ref,
    dk_ref,
    dv_ref,
    q_v,
    g_v,
    win,
    win_t,
    bias,
    s_ref,
    dp_ref,
    w_ref,
    ds_ref,
    acc,
    own,
    out_part,
    in_part,
    load_sem,
    own_sem,
    send_sem,
    recv_sem,
    back_send,
    back_recv,
):
    T = q_hbm.shape[0]
    W = SPAN * T
    WIN = W - SUB
    inner = lax.axis_size("inner")
    count = lax.axis_size("blk") * inner
    me = lax.axis_index("blk") * inner + lax.axis_index("inner")
    scale = 1.0 / math.sqrt(HEAD)
    cols = GROUP * HEAD

    def device(offset):
        there = lax.rem(me + offset + count, count)
        return (there // inner, lax.rem(there, inner))

    def load(j, which):
        src, dst = ((q_hbm, q_v), (g_hbm, g_v))[which]
        at = pl.ds(pl.multiple_of(j * cols, cols), cols)
        return pltpu.make_async_copy(src.at[:, at], dst.at[j], load_sem.at[j, which])

    def own_copy(j, which):
        src = (k_hbm, v_hbm)[which]
        at = pl.ds(pl.multiple_of(j * HEAD, HEAD), HEAD)
        return pltpu.make_async_copy(
            src.at[:, at], win.at[which, j, pl.ds(W - T, T), :], own_sem.at[j, which]
        )

    def send(j, d, which):
        src = (k_hbm, v_hbm)[which]
        at = pl.ds(pl.multiple_of(j * HEAD, HEAD), HEAD)
        return pltpu.make_async_remote_copy(
            src_ref=src.at[:, at],
            dst_ref=win.at[which, j, pl.ds((SPAN - 1 - d) * T, T), :],
            send_sem=send_sem.at[j, d - 1, which],
            recv_sem=recv_sem.at[j, d - 1, which],
            device_id=device(d),
            device_id_type=MESH,
        )

    def back(j, d, which):
        return pltpu.make_async_remote_copy(
            src_ref=out_part.at[which, j, pl.ds((SPAN - 1 - d) * T, T), :],
            dst_ref=in_part.at[which, j, d - 1],
            send_sem=back_send.at[j, d - 1, which],
            recv_sem=back_recv.at[j, d - 1, which],
            device_id=device(-d),
            device_id_type=MESH,
        )

    def each(fn):
        for d in range(1, SPAN):
            for which in range(2):
                fn(d, which)

    barrier = pltpu.get_barrier_semaphore()
    for d in range(1, SPAN):
        for sign in (1, -1):
            pl.semaphore_signal(barrier, inc=1, device_id=device(sign * d), device_id_type=MESH)

    @pl.loop(0, KV_HEADS)
    def _(j):
        for which in range(2):
            own_copy(j, which).start()
            load(j, which).start()

    pl.semaphore_wait(barrier, 2 * (SPAN - 1))
    each(lambda d, which: send(0, d, which).start())

    q_pos = me * T + lax.broadcasted_iota(jnp.int32, (8, T), 1)

    def doc_step(i, carry):
        end, first = carry
        end = end + len_ref[i]
        return end, jnp.where(q_pos >= end, end, first)

    _, first = lax.fori_loop(
        0, len_ref.shape[0], doc_step, (jnp.int32(0), jnp.zeros((8, T), jnp.int32))
    )
    for sub in range(T // SUB):
        low = first[0:1, sub * SUB : (sub + 1) * SUB]
        high = q_pos[0:1, sub * SUB : (sub + 1) * SUB]
        start = (me - (SPAN - 1)) * T + sub * SUB
        for c in range(WIN // SUB):
            k_pos = start + c * SUB + lax.broadcasted_iota(jnp.int32, (SUB, SUB), 0)
            ok = (k_pos >= low) & (k_pos <= high)
            bias[sub, c * SUB : (c + 1) * SUB, :] = jnp.where(ok, 0.0, -1e30)

    @pl.loop(0, KV_HEADS)
    def _(j):
        @pl.when(j + 1 < KV_HEADS)
        def _():
            each(lambda d, which: send(j + 1, d, which).start())

        for which in range(2):
            own_copy(j, which).wait()
            load(j, which).wait()
        each(lambda d, which: send(j, d, which).wait_recv())
        for which in range(2):
            for r in range(0, W, SUB):
                win_t[which, :, r : r + SUB] = win[which, j, r : r + SUB, :].T
        acc[...] = jnp.zeros_like(acc)

        def unit(pair, sub):
            rows = slice(sub * SUB, (sub + 1) * SUB)
            col0 = pl.ds(pl.multiple_of(pair * 2 * HEAD, HEAD), HEAD)
            col1 = pl.ds(pl.multiple_of(pair * 2 * HEAD + HEAD, HEAD), HEAD)
            out0 = pl.ds(pl.multiple_of(j * cols + pair * 2 * HEAD, HEAD), HEAD)
            out1 = pl.ds(pl.multiple_of(j * cols + pair * 2 * HEAD + HEAD, HEAD), HEAD)
            qu = jnp.concatenate([q_v[j, rows, col0], q_v[j, rows, col1]], axis=0)
            gu = jnp.concatenate([g_v[j, rows, col0], g_v[j, rows, col1]], axis=0)

            def keys(c):
                return slice((sub + c) * SUB, (sub + c + 1) * SUB)

            top = None
            for c in range(WIN // SUB):
                at = slice(c * SUB, (c + 1) * SUB)
                extra = bias[sub, at, :]
                s = dot(win[0, j, keys(c), :], qu, NT) + jnp.concatenate([extra, extra], axis=1)
                s_ref[at, :] = s
                part = fold_rows(s, jnp.maximum)
                top = part if top is None else jnp.maximum(top, part)
            top = jnp.max(top, axis=0, keepdims=True)
            total = jnp.zeros((8, 2 * SUB), jnp.float32)
            cross = jnp.zeros((8, 2 * SUB), jnp.float32)
            for c in range(WIN // SUB):
                at = slice(c * SUB, (c + 1) * SUB)
                p = jnp.exp2((s_ref[at, :] - top) * (scale * math.log2(math.e)))
                dp = dot(win[1, j, keys(c), :], gu, NT)
                total = total + fold_rows(p, jnp.add)
                cross = cross + fold_rows(p * dp, jnp.add)
                s_ref[at, :] = p
                dp_ref[at, :] = dp
            inv = 1.0 / jnp.sum(total, axis=0, keepdims=True)
            delta = jnp.sum(cross, axis=0, keepdims=True) * inv
            for c in range(WIN // SUB):
                at = slice(c * SUB, (c + 1) * SUB)
                w = s_ref[at, :] * inv
                w_ref[at, :] = w.astype(jnp.bfloat16)
                ds_ref[at, :] = (w * (dp_ref[at, :] - delta)).astype(jnp.bfloat16)
            span = slice(sub * SUB, sub * SUB + WIN)
            o_t = dot(win_t[1, :, span], w_ref[...], NN)
            dq_t = dot(win_t[0, :, span], ds_ref[...], NN) * scale
            att_ref[rows, out0] = o_t[:, :SUB].T.astype(jnp.bfloat16)
            att_ref[rows, out1] = o_t[:, SUB:].T.astype(jnp.bfloat16)
            dq_ref[rows, out0] = dq_t[:, :SUB].T.astype(jnp.bfloat16)
            dq_ref[rows, out1] = dq_t[:, SUB:].T.astype(jnp.bfloat16)
            acc[0, span, :] += dot(ds_ref[...], qu, NN)
            acc[1, span, :] += dot(w_ref[...], gu, NN)

        @pl.loop(0, GROUP // 2)
        def _(pair):
            for sub in range(T // SUB):
                unit(pair, sub)

        for which in range(2):
            factor = scale if which == 0 else 1.0
            out_part[which, j] = (acc[which, : W - T, :] * factor).astype(jnp.bfloat16)
            own[which, j] = acc[which, W - T :, :] * factor
        each(lambda d, which: back(j, d, which).start())

    @pl.loop(0, KV_HEADS)
    def _(j):
        each(lambda d, which: back(j, d, which).wait_recv())
        at = pl.ds(pl.multiple_of(j * HEAD, HEAD), HEAD)
        for which, ref in ((0, dk_ref), (1, dv_ref)):
            sums = own[which, j]
            for d in range(1, SPAN):
                sums = sums + in_part[which, j, d - 1].astype(jnp.float32)
            ref[:, at] = sums.astype(jnp.bfloat16)

    @pl.loop(0, KV_HEADS)
    def _(j):
        each(lambda d, which: send(j, d, which).wait_send())
        each(lambda d, which: back(j, d, which).wait_send())


def local(queries, keys, values, out_grad, doc_lengths):
    T = queries.shape[0]
    W = SPAN * T
    WIN = W - SUB
    bf16, f32 = jnp.bfloat16, jnp.float32
    anywhere = pl.BlockSpec(memory_space=pl.ANY)
    vmem = pl.BlockSpec(memory_space=pltpu.VMEM)
    dma = pltpu.SemaphoreType.DMA
    return pl.pallas_call(
        kernel,
        out_shape=(
            jax.ShapeDtypeStruct(queries.shape, bf16),
            jax.ShapeDtypeStruct(queries.shape, bf16),
            jax.ShapeDtypeStruct(keys.shape, bf16),
            jax.ShapeDtypeStruct(keys.shape, bf16),
        ),
        in_specs=[anywhere] * 4 + [pl.BlockSpec(memory_space=pltpu.SMEM)],
        out_specs=(vmem, vmem, vmem, vmem),
        scratch_shapes=[
            pltpu.VMEM((KV_HEADS, T, GROUP * HEAD), bf16),
            pltpu.VMEM((KV_HEADS, T, GROUP * HEAD), bf16),
            pltpu.VMEM((2, KV_HEADS, W, HEAD), bf16),
            pltpu.VMEM((2, HEAD, W), bf16),
            pltpu.VMEM((T // SUB, WIN, SUB), f32),
            pltpu.VMEM((WIN, 2 * SUB), f32),
            pltpu.VMEM((WIN, 2 * SUB), f32),
            pltpu.VMEM((WIN, 2 * SUB), bf16),
            pltpu.VMEM((WIN, 2 * SUB), bf16),
            pltpu.VMEM((2, W, HEAD), f32),
            pltpu.VMEM((2, KV_HEADS, T, HEAD), f32),
            pltpu.VMEM((2, KV_HEADS, W - T, HEAD), bf16),
            pltpu.VMEM((2, KV_HEADS, SPAN - 1, T, HEAD), bf16),
            dma((KV_HEADS, 2)),
            dma((KV_HEADS, 2)),
            dma((KV_HEADS, SPAN - 1, 2)),
            dma((KV_HEADS, SPAN - 1, 2)),
            dma((KV_HEADS, SPAN - 1, 2)),
            dma((KV_HEADS, SPAN - 1, 2)),
        ],
        compiler_params=pltpu.CompilerParams(
            collective_id=0, has_side_effects=True, vmem_limit_bytes=48 * 1024 * 1024
        ),
        name="attention",
    )(queries, keys, values, out_grad, doc_lengths)


def solution(mesh):
    rows = P(("blk", "inner"), None)
    return jax.shard_map(
        local,
        mesh=mesh,
        in_specs=(rows, rows, rows, rows, P()),
        out_specs=(rows, rows, rows, rows),
        check_vma=False,
    )
```

```python
import math

import jax
import jax.numpy as jnp
from jax import lax
from jax.experimental import pallas as pl
from jax.experimental.pallas import tpu as pltpu
from jax.sharding import PartitionSpec as P

HEAD = 128
KV_HEADS = 4
GROUP = 8
SPAN = 4
RING = 4
SUB = 128
MESH = pl.DeviceIdType.MESH
NT = (((1,), (1,)), ((), ()))
NN = (((1,), (0,)), ((), ()))


def dot(a, b, dims):
    return lax.dot_general(a, b, dims, preferred_element_type=jnp.float32)


def fold_rows(x, op):
    rows = x.shape[0]
    parts = [x[r : r + 8] for r in range(0, rows, 8)]
    while len(parts) > 1:
        parts = [op(parts[i], parts[i + 1]) for i in range(0, len(parts), 2)]
    return parts[0]


def kernel(
    q_hbm,
    k_hbm,
    v_hbm,
    g_hbm,
    len_hbm,
    att_ref,
    dq_ref,
    dk_ref,
    dv_ref,
    q_v,
    g_v,
    win,
    win_t,
    bias,
    s_ref,
    dp_ref,
    w_ref,
    ds_ref,
    acc,
    own,
    out_part,
    in_part,
    relay_out,
    relay_in,
    len_ref,
    load_sem,
    own_sem,
    len_sem,
    cross_send,
    cross_recv,
    share_send,
    share_recv,
    back_send,
    back_recv,
    relay_send,
    relay_recv,
):
    T = q_hbm.shape[0]
    W = SPAN * T
    WIN = W - SUB
    inner = lax.axis_size("inner")
    count = lax.axis_size("blk") * inner
    me = lax.axis_index("blk") * inner + lax.axis_index("inner")
    scale = 1.0 / math.sqrt(HEAD)
    cols = GROUP * HEAD

    def device(offset):
        there = lax.rem(me + offset + count, count)
        return (there // inner, lax.rem(there, inner))

    place = lax.rem(me, RING)

    def member(offset):
        there = me - place + lax.rem(place + offset + RING, RING)
        return (there // inner, lax.rem(there, inner))

    def load(j, which):
        src, dst = ((q_hbm, q_v), (g_hbm, g_v))[which]
        at = pl.ds(pl.multiple_of(j * cols, cols), cols)
        return pltpu.make_async_copy(src.at[:, at], dst.at[j], load_sem.at[j, which])

    def own_copy(j, which):
        src = (k_hbm, v_hbm)[which]
        at = pl.ds(pl.multiple_of(j * HEAD, HEAD), HEAD)
        return pltpu.make_async_copy(
            src.at[:, at], win.at[which, j, pl.ds(W - T, T), :], own_sem.at[j, which]
        )

    def cross(j, which):
        return pltpu.make_async_remote_copy(
            src_ref=win.at[which, j, pl.ds(W - T, T), :],
            dst_ref=win.at[which, j, pl.ds(W, T), :],
            send_sem=cross_send.at[j, which],
            recv_sem=cross_recv.at[j, which],
            device_id=device(RING),
            device_id_type=MESH,
        )

    def share(j, m, which, relayed):
        return pltpu.make_async_remote_copy(
            src_ref=win.at[which, j, pl.ds(W if relayed else W - T, T), :],
            dst_ref=win.at[which, j, pl.ds((SPAN - 1 - m) * T, T), :],
            send_sem=share_send.at[j, m - 1, which],
            recv_sem=share_recv.at[j, m - 1, which],
            device_id=member(m),
            device_id_type=MESH,
        )

    def back(j, m, which):
        return pltpu.make_async_remote_copy(
            src_ref=out_part.at[which, j, pl.ds((SPAN - 1 - m) * T, T), :],
            dst_ref=in_part.at[which, j, m - 1],
            send_sem=back_send.at[j, m - 1, which],
            recv_sem=back_recv.at[j, m - 1, which],
            device_id=member(-m),
            device_id_type=MESH,
        )

    def cross_back(j, which):
        return pltpu.make_async_remote_copy(
            src_ref=relay_out.at[which, j],
            dst_ref=relay_in.at[which, j],
            send_sem=relay_send.at[j, which],
            recv_sem=relay_recv.at[j, which],
            device_id=device(-RING),
            device_id_type=MESH,
        )

    def each(fn):
        for m in range(1, SPAN):
            for which in range(2):
                fn(m, which)

    def start_shares(j):
        for m in range(1, SPAN):

            @pl.when(place + m < RING)
            def _():
                for which in range(2):
                    share(j, m, which, False).start()

        for which in range(2):
            cross(j, which).wait_recv()
        for m in range(1, SPAN):

            @pl.when(place + m >= RING)
            def _():
                for which in range(2):
                    share(j, m, which, True).start()

    barrier = pltpu.get_barrier_semaphore()
    for m in range(1, RING):
        pl.semaphore_signal(barrier, inc=1, device_id=member(m), device_id_type=MESH)
    for sign in (1, -1):
        pl.semaphore_signal(barrier, inc=1, device_id=device(sign * RING), device_id_type=MESH)

    @pl.loop(0, KV_HEADS)
    def _(j):
        for which in range(2):
            own_copy(j, which).start()

    lengths = pltpu.make_async_copy(len_hbm, len_ref, len_sem)
    lengths.start()

    @pl.loop(0, KV_HEADS)
    def _(j):
        for which in range(2):
            load(j, which).start()

    pl.semaphore_wait(barrier, RING + 1)

    @pl.loop(0, KV_HEADS)
    def _(j):
        for which in range(2):
            own_copy(j, which).wait()
            cross(j, which).start()

    start_shares(0)
    lengths.wait()

    q_pos = me * T + lax.broadcasted_iota(jnp.int32, (8, T), 1)

    def doc_step(i, carry):
        end, first = carry
        end = end + len_ref[i]
        return end, jnp.where(q_pos >= end, end, first)

    _, first = lax.fori_loop(
        0, len_ref.shape[0], doc_step, (jnp.int32(0), jnp.zeros((8, T), jnp.int32))
    )
    for sub in range(T // SUB):
        low = first[0:1, sub * SUB : (sub + 1) * SUB]
        high = q_pos[0:1, sub * SUB : (sub + 1) * SUB]
        start = (me - (SPAN - 1)) * T + sub * SUB
        for c in range(WIN // SUB):
            k_pos = start + c * SUB + lax.broadcasted_iota(jnp.int32, (SUB, SUB), 0)
            ok = (k_pos >= low) & (k_pos <= high)
            bias[sub, c * SUB : (c + 1) * SUB, :] = jnp.where(ok, 0.0, -1e30)

    def relay(j):
        each(lambda m, which: back(j, m, which).wait_recv())
        for which in range(2):
            mine = own[which, j]
            theirs = jnp.zeros((T, HEAD), jnp.float32)
            for m in range(1, SPAN):
                part = in_part[which, j, m - 1].astype(jnp.float32)
                keep = place + m < RING
                mine = mine + jnp.where(keep, part, 0.0)
                theirs = theirs + jnp.where(keep, 0.0, part)
            own[which, j] = mine
            relay_out[which, j] = theirs.astype(jnp.bfloat16)
            cross_back(j, which).start()

    @pl.loop(0, KV_HEADS)
    def _(j):
        @pl.when(j + 1 < KV_HEADS)
        def _():
            start_shares(j + 1)

        for which in range(2):
            load(j, which).wait()
        each(lambda m, which: share(j, m, which, False).wait_recv())
        for which in range(2):
            for r in range(0, W, SUB):
                win_t[which, :, r : r + SUB] = win[which, j, r : r + SUB, :].T
        acc[...] = jnp.zeros_like(acc)

        def unit(pair, sub):
            rows = slice(sub * SUB, (sub + 1) * SUB)
            col0 = pl.ds(pl.multiple_of(pair * 2 * HEAD, HEAD), HEAD)
            col1 = pl.ds(pl.multiple_of(pair * 2 * HEAD + HEAD, HEAD), HEAD)
            out0 = pl.ds(pl.multiple_of(j * cols + pair * 2 * HEAD, HEAD), HEAD)
            out1 = pl.ds(pl.multiple_of(j * cols + pair * 2 * HEAD + HEAD, HEAD), HEAD)
            qu = jnp.concatenate([q_v[j, rows, col0], q_v[j, rows, col1]], axis=0)
            gu = jnp.concatenate([g_v[j, rows, col0], g_v[j, rows, col1]], axis=0)

            def keys(c):
                return slice((sub + c) * SUB, (sub + c + 1) * SUB)

            top = None
            for c in range(WIN // SUB):
                at = slice(c * SUB, (c + 1) * SUB)
                extra = bias[sub, at, :]
                s = dot(win[0, j, keys(c), :], qu, NT) + jnp.concatenate([extra, extra], axis=1)
                s_ref[at, :] = s
                part = fold_rows(s, jnp.maximum)
                top = part if top is None else jnp.maximum(top, part)
            top = jnp.max(top, axis=0, keepdims=True)
            total = jnp.zeros((8, 2 * SUB), jnp.float32)
            cross = jnp.zeros((8, 2 * SUB), jnp.float32)
            for c in range(WIN // SUB):
                at = slice(c * SUB, (c + 1) * SUB)
                p = jnp.exp2((s_ref[at, :] - top) * (scale * math.log2(math.e)))
                dp = dot(win[1, j, keys(c), :], gu, NT)
                total = total + fold_rows(p, jnp.add)
                cross = cross + fold_rows(p * dp, jnp.add)
                s_ref[at, :] = p
                dp_ref[at, :] = dp
            inv = 1.0 / jnp.sum(total, axis=0, keepdims=True)
            delta = jnp.sum(cross, axis=0, keepdims=True) * inv
            for c in range(WIN // SUB):
                at = slice(c * SUB, (c + 1) * SUB)
                w = s_ref[at, :] * inv
                w_ref[at, :] = w.astype(jnp.bfloat16)
                ds_ref[at, :] = (w * (dp_ref[at, :] - delta)).astype(jnp.bfloat16)
            span = slice(sub * SUB, sub * SUB + WIN)
            o_t = dot(win_t[1, :, span], w_ref[...], NN)
            dq_t = dot(win_t[0, :, span], ds_ref[...], NN) * scale
            att_ref[rows, out0] = o_t[:, :SUB].T.astype(jnp.bfloat16)
            att_ref[rows, out1] = o_t[:, SUB:].T.astype(jnp.bfloat16)
            dq_ref[rows, out0] = dq_t[:, :SUB].T.astype(jnp.bfloat16)
            dq_ref[rows, out1] = dq_t[:, SUB:].T.astype(jnp.bfloat16)
            acc[0, span, :] += dot(ds_ref[...], qu, NN)
            acc[1, span, :] += dot(w_ref[...], gu, NN)

        @pl.loop(0, GROUP // 2)
        def _(pair):
            for sub in range(T // SUB):
                unit(pair, sub)

        for which in range(2):
            factor = scale if which == 0 else 1.0
            out_part[which, j] = (acc[which, : W - T, :] * factor).astype(jnp.bfloat16)
            own[which, j] = acc[which, W - T :, :] * factor
        each(lambda m, which: back(j, m, which).start())

        @pl.when(j > 0)
        def _():
            relay(j - 1)

    relay(KV_HEADS - 1)

    @pl.loop(0, KV_HEADS)
    def _(j):
        at = pl.ds(pl.multiple_of(j * HEAD, HEAD), HEAD)
        for which, ref in ((0, dk_ref), (1, dv_ref)):
            cross_back(j, which).wait_recv()
            sums = own[which, j] + relay_in[which, j].astype(jnp.float32)
            ref[:, at] = sums.astype(jnp.bfloat16)

    @pl.loop(0, KV_HEADS)
    def _(j):
        each(lambda m, which: share(j, m, which, False).wait_send())
        each(lambda m, which: back(j, m, which).wait_send())
        for which in range(2):
            cross(j, which).wait_send()
            cross_back(j, which).wait_send()


def local(queries, keys, values, out_grad, doc_lengths):
    T = queries.shape[0]
    W = SPAN * T
    WIN = W - SUB
    bf16, f32 = jnp.bfloat16, jnp.float32
    hbm = pl.BlockSpec(memory_space=pltpu.HBM)
    vmem = pl.BlockSpec(memory_space=pltpu.VMEM)
    dma = pltpu.SemaphoreType.DMA
    return pl.pallas_call(
        kernel,
        out_shape=(
            jax.ShapeDtypeStruct(queries.shape, bf16),
            jax.ShapeDtypeStruct(queries.shape, bf16),
            jax.ShapeDtypeStruct(keys.shape, bf16),
            jax.ShapeDtypeStruct(keys.shape, bf16),
        ),
        in_specs=[hbm] * 5,
        out_specs=(vmem, vmem, vmem, vmem),
        scratch_shapes=[
            pltpu.VMEM((KV_HEADS, T, GROUP * HEAD), bf16),
            pltpu.VMEM((KV_HEADS, T, GROUP * HEAD), bf16),
            pltpu.VMEM((2, KV_HEADS, W + T, HEAD), bf16),
            pltpu.VMEM((2, HEAD, W), bf16),
            pltpu.VMEM((T // SUB, WIN, SUB), f32),
            pltpu.VMEM((WIN, 2 * SUB), f32),
            pltpu.VMEM((WIN, 2 * SUB), f32),
            pltpu.VMEM((WIN, 2 * SUB), bf16),
            pltpu.VMEM((WIN, 2 * SUB), bf16),
            pltpu.VMEM((2, W, HEAD), f32),
            pltpu.VMEM((2, KV_HEADS, T, HEAD), f32),
            pltpu.VMEM((2, KV_HEADS, W - T, HEAD), bf16),
            pltpu.VMEM((2, KV_HEADS, SPAN - 1, T, HEAD), bf16),
            pltpu.VMEM((2, KV_HEADS, T, HEAD), bf16),
            pltpu.VMEM((2, KV_HEADS, T, HEAD), bf16),
            pltpu.SMEM(doc_lengths.shape, jnp.int32),
            dma((KV_HEADS, 2)),
            dma((KV_HEADS, 2)),
            dma(()),
            dma((KV_HEADS, 2)),
            dma((KV_HEADS, 2)),
            dma((KV_HEADS, SPAN - 1, 2)),
            dma((KV_HEADS, SPAN - 1, 2)),
            dma((KV_HEADS, SPAN - 1, 2)),
            dma((KV_HEADS, SPAN - 1, 2)),
            dma((KV_HEADS, 2)),
            dma((KV_HEADS, 2)),
        ],
        compiler_params=pltpu.CompilerParams(
            collective_id=0, has_side_effects=True, vmem_limit_bytes=48 * 1024 * 1024
        ),
        name="attention",
    )(queries, keys, values, out_grad, doc_lengths)


def solution(mesh):
    rows = P(("blk", "inner"), None)
    return jax.shard_map(
        local,
        mesh=mesh,
        in_specs=(rows, rows, rows, rows, P()),
        out_specs=(rows, rows, rows, rows),
        check_vma=False,
    )
```

```python
import math

import jax
import jax.numpy as jnp
from jax import lax
from jax.experimental import pallas as pl
from jax.experimental.pallas import tpu as pltpu
from jax.sharding import PartitionSpec as P

HEAD = 128
KV_HEADS = 4
GROUP = 8
SPAN = 4
SUB = 128
MESH = pl.DeviceIdType.MESH
NT = (((1,), (1,)), ((), ()))
NN = (((1,), (0,)), ((), ()))


def dot(a, b, dims):
    return lax.dot_general(a, b, dims, preferred_element_type=jnp.float32)


def fold_rows(x, op):
    rows = x.shape[0]
    parts = [x[r : r + 8] for r in range(0, rows, 8)]
    while len(parts) > 1:
        parts = [op(parts[i], parts[i + 1]) for i in range(0, len(parts), 2)]
    return parts[0]


def kernel(
    q_hbm,
    k_hbm,
    v_hbm,
    g_hbm,
    len_hbm,
    att_ref,
    dq_ref,
    dk_ref,
    dv_ref,
    q_v,
    g_v,
    win,
    win_t,
    bias,
    s_ref,
    dp_ref,
    w_ref,
    ds_ref,
    acc,
    own,
    out_part,
    in_part,
    len_ref,
    len_sem,
    load_sem,
    own_sem,
    send_sem,
    recv_sem,
    back_send,
    back_recv,
):
    T = q_hbm.shape[0]
    W = SPAN * T
    WIN = W - SUB
    inner = lax.axis_size("inner")
    count = lax.axis_size("blk") * inner
    me = lax.axis_index("blk") * inner + lax.axis_index("inner")
    scale = 1.0 / math.sqrt(HEAD)
    cols = GROUP * HEAD

    def device(offset):
        there = lax.rem(me + offset + count, count)
        return (there // inner, lax.rem(there, inner))

    def load(j, which):
        src, dst = ((q_hbm, q_v), (g_hbm, g_v))[which]
        at = pl.ds(pl.multiple_of(j * cols, cols), cols)
        return pltpu.make_async_copy(src.at[:, at], dst.at[j], load_sem.at[j, which])

    def own_copy(j, which):
        src = (k_hbm, v_hbm)[which]
        at = pl.ds(pl.multiple_of(j * HEAD, HEAD), HEAD)
        return pltpu.make_async_copy(
            src.at[:, at], win.at[which, j, pl.ds(W - T, T), :], own_sem.at[j, which]
        )

    def send(j, d, which):
        src = (k_hbm, v_hbm)[which]
        at = pl.ds(pl.multiple_of(j * HEAD, HEAD), HEAD)
        return pltpu.make_async_remote_copy(
            src_ref=src.at[:, at],
            dst_ref=win.at[which, j, pl.ds((SPAN - 1 - d) * T, T), :],
            send_sem=send_sem.at[j, d - 1, which],
            recv_sem=recv_sem.at[j, d - 1, which],
            device_id=device(d),
            device_id_type=MESH,
        )

    def back(j, d, which):
        return pltpu.make_async_remote_copy(
            src_ref=out_part.at[which, j, pl.ds((SPAN - 1 - d) * T, T), :],
            dst_ref=in_part.at[which, j, d - 1],
            send_sem=back_send.at[j, d - 1, which],
            recv_sem=back_recv.at[j, d - 1, which],
            device_id=device(-d),
            device_id_type=MESH,
        )

    def each(fn):
        for d in range(1, SPAN):
            for which in range(2):
                fn(d, which)

    barrier = pltpu.get_barrier_semaphore()
    for d in range(1, SPAN):
        for sign in (1, -1):
            pl.semaphore_signal(barrier, inc=1, device_id=device(sign * d), device_id_type=MESH)

    lengths = pltpu.make_async_copy(len_hbm, len_ref, len_sem)
    lengths.start()

    @pl.loop(0, KV_HEADS)
    def _(j):
        for which in range(2):
            own_copy(j, which).start()
            load(j, which).start()

    pl.semaphore_wait(barrier, 2 * (SPAN - 1))
    each(lambda d, which: send(0, d, which).start())

    lengths.wait()

    q_pos = me * T + lax.broadcasted_iota(jnp.int32, (8, T), 1)

    def doc_step(i, carry):
        end, first = carry
        end = end + len_ref[i]
        return end, jnp.where(q_pos >= end, end, first)

    _, first = lax.fori_loop(
        0, len_ref.shape[0], doc_step, (jnp.int32(0), jnp.zeros((8, T), jnp.int32))
    )
    for sub in range(T // SUB):
        low = first[0:1, sub * SUB : (sub + 1) * SUB]
        high = q_pos[0:1, sub * SUB : (sub + 1) * SUB]
        start = (me - (SPAN - 1)) * T + sub * SUB
        for c in range(WIN // SUB):
            k_pos = start + c * SUB + lax.broadcasted_iota(jnp.int32, (SUB, SUB), 0)
            ok = (k_pos >= low) & (k_pos <= high)
            bias[sub, c * SUB : (c + 1) * SUB, :] = jnp.where(ok, 0.0, -1e30)

    @pl.loop(0, KV_HEADS)
    def _(j):
        @pl.when(j + 1 < KV_HEADS)
        def _():
            each(lambda d, which: send(j + 1, d, which).start())

        for which in range(2):
            own_copy(j, which).wait()
            load(j, which).wait()
        each(lambda d, which: send(j, d, which).wait_recv())
        for which in range(2):
            for r in range(0, W, SUB):
                win_t[which, :, r : r + SUB] = win[which, j, r : r + SUB, :].T
        acc[...] = jnp.zeros_like(acc)

        def unit(pair, sub):
            rows = slice(sub * SUB, (sub + 1) * SUB)
            col0 = pl.ds(pl.multiple_of(pair * 2 * HEAD, HEAD), HEAD)
            col1 = pl.ds(pl.multiple_of(pair * 2 * HEAD + HEAD, HEAD), HEAD)
            out0 = pl.ds(pl.multiple_of(j * cols + pair * 2 * HEAD, HEAD), HEAD)
            out1 = pl.ds(pl.multiple_of(j * cols + pair * 2 * HEAD + HEAD, HEAD), HEAD)
            qu = jnp.concatenate([q_v[j, rows, col0], q_v[j, rows, col1]], axis=0)
            gu = jnp.concatenate([g_v[j, rows, col0], g_v[j, rows, col1]], axis=0)

            def keys(c):
                return slice((sub + c) * SUB, (sub + c + 1) * SUB)

            top = None
            for c in range(WIN // SUB):
                at = slice(c * SUB, (c + 1) * SUB)
                extra = bias[sub, at, :]
                s = dot(win[0, j, keys(c), :], qu, NT) + jnp.concatenate([extra, extra], axis=1)
                s_ref[at, :] = s
                part = fold_rows(s, jnp.maximum)
                top = part if top is None else jnp.maximum(top, part)
            top = jnp.max(top, axis=0, keepdims=True)
            total = jnp.zeros((8, 2 * SUB), jnp.float32)
            cross = jnp.zeros((8, 2 * SUB), jnp.float32)
            for c in range(WIN // SUB):
                at = slice(c * SUB, (c + 1) * SUB)
                p = jnp.exp2((s_ref[at, :] - top) * (scale * math.log2(math.e)))
                dp = dot(win[1, j, keys(c), :], gu, NT)
                total = total + fold_rows(p, jnp.add)
                cross = cross + fold_rows(p * dp, jnp.add)
                s_ref[at, :] = p
                dp_ref[at, :] = dp
            inv = 1.0 / jnp.sum(total, axis=0, keepdims=True)
            delta = jnp.sum(cross, axis=0, keepdims=True) * inv
            for c in range(WIN // SUB):
                at = slice(c * SUB, (c + 1) * SUB)
                w = s_ref[at, :] * inv
                w_ref[at, :] = w.astype(jnp.bfloat16)
                ds_ref[at, :] = (w * (dp_ref[at, :] - delta)).astype(jnp.bfloat16)
            span = slice(sub * SUB, sub * SUB + WIN)
            o_t = dot(win_t[1, :, span], w_ref[...], NN)
            dq_t = dot(win_t[0, :, span], ds_ref[...], NN) * scale
            att_ref[rows, out0] = o_t[:, :SUB].T.astype(jnp.bfloat16)
            att_ref[rows, out1] = o_t[:, SUB:].T.astype(jnp.bfloat16)
            dq_ref[rows, out0] = dq_t[:, :SUB].T.astype(jnp.bfloat16)
            dq_ref[rows, out1] = dq_t[:, SUB:].T.astype(jnp.bfloat16)
            acc[0, span, :] += dot(ds_ref[...], qu, NN)
            acc[1, span, :] += dot(w_ref[...], gu, NN)

        @pl.loop(0, GROUP // 2)
        def _(pair):
            for sub in range(T // SUB):
                unit(pair, sub)

        for which in range(2):
            factor = scale if which == 0 else 1.0
            out_part[which, j] = (acc[which, : W - T, :] * factor).astype(jnp.bfloat16)
            own[which, j] = acc[which, W - T :, :] * factor
        each(lambda d, which: back(j, d, which).start())

    @pl.loop(0, KV_HEADS)
    def _(j):
        each(lambda d, which: back(j, d, which).wait_recv())
        at = pl.ds(pl.multiple_of(j * HEAD, HEAD), HEAD)
        for which, ref in ((0, dk_ref), (1, dv_ref)):
            sums = own[which, j]
            for d in range(1, SPAN):
                sums = sums + in_part[which, j, d - 1].astype(jnp.float32)
            ref[:, at] = sums.astype(jnp.bfloat16)

    @pl.loop(0, KV_HEADS)
    def _(j):
        each(lambda d, which: send(j, d, which).wait_send())
        each(lambda d, which: back(j, d, which).wait_send())


def place_results(*refs):
    sem = refs[-1]
    copies = [pltpu.make_async_copy(refs[i], refs[4 + i], sem.at[i]) for i in range(4)]
    for copy in copies:
        copy.start()
    for copy in copies:
        copy.wait()


def local(queries, keys, values, out_grad, doc_lengths):
    T = queries.shape[0]
    W = SPAN * T
    WIN = W - SUB
    bf16, f32 = jnp.bfloat16, jnp.float32
    anywhere = pl.BlockSpec(memory_space=pl.ANY)
    vmem = pl.BlockSpec(memory_space=pltpu.VMEM)
    dma = pltpu.SemaphoreType.DMA
    parts = pl.pallas_call(
        kernel,
        out_shape=(
            jax.ShapeDtypeStruct(queries.shape, bf16),
            jax.ShapeDtypeStruct(queries.shape, bf16),
            jax.ShapeDtypeStruct(keys.shape, bf16),
            jax.ShapeDtypeStruct(keys.shape, bf16),
        ),
        in_specs=[anywhere] * 5,
        out_specs=(vmem, vmem, vmem, vmem),
        scratch_shapes=[
            pltpu.VMEM((KV_HEADS, T, GROUP * HEAD), bf16),
            pltpu.VMEM((KV_HEADS, T, GROUP * HEAD), bf16),
            pltpu.VMEM((2, KV_HEADS, W, HEAD), bf16),
            pltpu.VMEM((2, HEAD, W), bf16),
            pltpu.VMEM((T // SUB, WIN, SUB), f32),
            pltpu.VMEM((WIN, 2 * SUB), f32),
            pltpu.VMEM((WIN, 2 * SUB), f32),
            pltpu.VMEM((WIN, 2 * SUB), bf16),
            pltpu.VMEM((WIN, 2 * SUB), bf16),
            pltpu.VMEM((2, W, HEAD), f32),
            pltpu.VMEM((2, KV_HEADS, T, HEAD), f32),
            pltpu.VMEM((2, KV_HEADS, W - T, HEAD), bf16),
            pltpu.VMEM((2, KV_HEADS, SPAN - 1, T, HEAD), bf16),
            pltpu.SMEM(doc_lengths.shape, jnp.int32),
            dma(()),
            dma((KV_HEADS, 2)),
            dma((KV_HEADS, 2)),
            dma((KV_HEADS, SPAN - 1, 2)),
            dma((KV_HEADS, SPAN - 1, 2)),
            dma((KV_HEADS, SPAN - 1, 2)),
            dma((KV_HEADS, SPAN - 1, 2)),
        ],
        compiler_params=pltpu.CompilerParams(
            collective_id=0, has_side_effects=True, vmem_limit_bytes=48 * 1024 * 1024
        ),
        name="attention",
    )(
        *(
            pltpu.with_memory_space_constraint(x, pltpu.HBM)
            for x in (queries, keys, values, out_grad, doc_lengths)
        )
    )
    return pl.pallas_call(
        place_results,
        out_shape=tuple(jax.ShapeDtypeStruct(x.shape, x.dtype) for x in parts),
        in_specs=[vmem] * 4,
        out_specs=(anywhere,) * 4,
        scratch_shapes=[dma((4,))],
        compiler_params=pltpu.CompilerParams(vmem_limit_bytes=1024 * 1024),
        name="results",
    )(*(pltpu.with_memory_space_constraint(x, pltpu.VMEM) for x in parts))


def solution(mesh):
    rows = P(("blk", "inner"), None)
    return jax.shard_map(
        local,
        mesh=mesh,
        in_specs=(rows, rows, rows, rows, P()),
        out_specs=(rows, rows, rows, rows),
        check_vma=False,
    )
```

```python
import math

import jax
import jax.numpy as jnp
from jax import lax
from jax.experimental import pallas as pl
from jax.experimental.pallas import tpu as pltpu
from jax.sharding import PartitionSpec as P

HEAD = 128
KV_HEADS = 4
GROUP = 8
SPAN = 4
SUB = 128
PATTERN = "bbabbabbababaaba"
AH = 4
BH = 7
MESH = pl.DeviceIdType.MESH
NT = (((1,), (1,)), ((), ()))
NN = (((1,), (0,)), ((), ()))


def dot(a, b, dims):
    return lax.dot_general(a, b, dims, preferred_element_type=jnp.float32)


def fold_rows(x, op):
    rows = x.shape[0]
    parts = [x[r : r + 8] for r in range(0, rows, 8)]
    while len(parts) > 1:
        parts = [op(parts[i], parts[i + 1]) for i in range(0, len(parts), 2)]
    return parts[0]


def kernel(
    q_hbm,
    k_hbm,
    v_hbm,
    g_hbm,
    len_hbm,
    att_ref,
    dq_ref,
    dk_ref,
    dv_ref,
    q_v,
    g_v,
    win,
    win_t,
    bias,
    p_ref,
    dp_ref,
    stats,
    w_ref,
    ds_ref,
    acc,
    own,
    out_part,
    in_part,
    len_ref,
    len_sem,
    load_sem,
    own_sem,
    send_sem,
    recv_sem,
    back_send,
    back_recv,
):
    T = q_hbm.shape[0]
    W = SPAN * T
    WIN = W - SUB
    inner = lax.axis_size("inner")
    count = lax.axis_size("blk") * inner
    me = lax.axis_index("blk") * inner + lax.axis_index("inner")
    scale = 1.0 / math.sqrt(HEAD)
    cols = GROUP * HEAD

    def device(offset):
        there = lax.rem(me + offset + count, count)
        return (there // inner, lax.rem(there, inner))

    def load(j, which):
        src, dst = ((q_hbm, q_v), (g_hbm, g_v))[which]
        at = pl.ds(pl.multiple_of(j * cols, cols), cols)
        return pltpu.make_async_copy(src.at[:, at], dst.at[j], load_sem.at[j, which])

    def own_copy(j, which):
        src = (k_hbm, v_hbm)[which]
        at = pl.ds(pl.multiple_of(j * HEAD, HEAD), HEAD)
        return pltpu.make_async_copy(
            src.at[:, at], win.at[which, j, pl.ds(W - T, T), :], own_sem.at[j, which]
        )

    def send(j, d, which):
        src = (k_hbm, v_hbm)[which]
        at = pl.ds(pl.multiple_of(j * HEAD, HEAD), HEAD)
        return pltpu.make_async_remote_copy(
            src_ref=src.at[:, at],
            dst_ref=win.at[which, j, pl.ds((SPAN - 1 - d) * T, T), :],
            send_sem=send_sem.at[j, d - 1, which],
            recv_sem=recv_sem.at[j, d - 1, which],
            device_id=device(d),
            device_id_type=MESH,
        )

    def back(j, d, which):
        return pltpu.make_async_remote_copy(
            src_ref=out_part.at[which, j, pl.ds((SPAN - 1 - d) * T, T), :],
            dst_ref=in_part.at[which, j, d - 1],
            send_sem=back_send.at[j, d - 1, which],
            recv_sem=back_recv.at[j, d - 1, which],
            device_id=device(-d),
            device_id_type=MESH,
        )

    def each(fn):
        for d in range(1, SPAN):
            for which in range(2):
                fn(d, which)

    barrier = pltpu.get_barrier_semaphore()
    for d in range(1, SPAN):
        for sign in (1, -1):
            pl.semaphore_signal(barrier, inc=1, device_id=device(sign * d), device_id_type=MESH)

    lengths = pltpu.make_async_copy(len_hbm, len_ref, len_sem)
    lengths.start()

    @pl.loop(0, KV_HEADS)
    def _(j):
        for which in range(2):
            own_copy(j, which).start()
            load(j, which).start()

    pl.semaphore_wait(barrier, 2 * (SPAN - 1))
    each(lambda d, which: send(0, d, which).start())

    lengths.wait()
    q_pos = me * T + lax.broadcasted_iota(jnp.int32, (8, T), 1)

    def doc_step(i, carry):
        end, first = carry
        end = end + len_ref[i]
        return end, jnp.where(q_pos >= end, end, first)

    _, first = lax.fori_loop(
        0, len_ref.shape[0], doc_step, (jnp.int32(0), jnp.zeros((8, T), jnp.int32))
    )
    for sub in range(T // SUB):
        low = first[0:1, sub * SUB : (sub + 1) * SUB]
        high = q_pos[0:1, sub * SUB : (sub + 1) * SUB]
        start = (me - (SPAN - 1)) * T + sub * SUB
        for c in range(WIN // SUB):
            k_pos = start + c * SUB + lax.broadcasted_iota(jnp.int32, (SUB, SUB), 0)
            ok = (k_pos >= low) & (k_pos <= high)
            bias[sub, c * SUB : (c + 1) * SUB, :] = jnp.where(ok, 0.0, -1e30)

    chunks = WIN // SUB
    to_exp2 = scale * math.log2(math.e)

    def arrive(j):
        each(lambda d, which: send(j, d, which).wait_recv())

    def stacked(ref, j, pair, sub):
        rows = slice(sub * SUB, (sub + 1) * SUB)
        parts = [
            ref[j, rows, pl.ds(pl.multiple_of((pair * 2 + side) * HEAD, HEAD), HEAD)]
            for side in range(2)
        ]
        return jnp.concatenate(parts, axis=0)

    def ahead(j, pair, sub):
        qu, gu = stacked(q_v, j, pair, sub), stacked(g_v, j, pair, sub)
        for c in range(chunks):
            at = slice(c * SUB, (c + 1) * SUB)
            keys = slice((sub + c) * SUB, (sub + c + 1) * SUB)
            extra = bias[sub, at, :]
            if c % AH == 0:
                wide = slice((sub + c) * SUB, (sub + min(c + AH, chunks)) * SUB)
                s_wide = dot(win[0, j, wide, :], qu, NT)
                dp_wide = dot(win[1, j, wide, :], gu, NT)
            part = slice(c % AH * SUB, (c % AH + 1) * SUB)
            s = s_wide[part] + jnp.concatenate([extra, extra], axis=1)
            dp = dp_wide[part]
            top = jnp.max(fold_rows(s, jnp.maximum), axis=0, keepdims=True)
            p = jnp.exp2((s - top) * to_exp2)
            p_ref[sub, at, :] = p
            dp_ref[sub, at, :] = dp
            stats[sub, 0, c] = jnp.broadcast_to(top, (8, 2 * SUB))
            stats[sub, 1, c] = fold_rows(p, jnp.add)
            stats[sub, 2, c] = fold_rows(p * dp, jnp.add)
            yield

    def behind(j, pair, sub):
        qu, gu = stacked(q_v, j, pair, sub), stacked(g_v, j, pair, sub)
        rows = slice(sub * SUB, (sub + 1) * SUB)
        tops = [stats[sub, 0, c] for c in range(chunks)]
        top = tops[0]
        for c in range(1, chunks):
            top = jnp.maximum(top, tops[c])
        factors = [jnp.exp2((tops[c] - top) * to_exp2) for c in range(chunks)]
        total = sum(stats[sub, 1, c] * factors[c] for c in range(chunks))
        cross = sum(stats[sub, 2, c] * factors[c] for c in range(chunks))
        inv = 1.0 / jnp.sum(total, axis=0, keepdims=True)
        delta = jnp.sum(cross, axis=0, keepdims=True) * inv
        for c in range(chunks):
            at = slice(c * SUB, (c + 1) * SUB)
            keys = slice((sub + c) * SUB, (sub + c + 1) * SUB)
            w = p_ref[sub, at, :] * (factors[c][0:1] * inv)
            ds = (w * (dp_ref[sub, at, :] - delta)).astype(jnp.bfloat16)
            w = w.astype(jnp.bfloat16)
            w_ref[sub, at, :] = w
            ds_ref[sub, at, :] = ds
            if (c + 1) % BH == 0 or c + 1 == chunks:
                low = c // BH * BH
                wide = slice((sub + low) * SUB, (sub + c + 1) * SUB)
                acc[0, wide, :] += dot(ds_ref[sub, low * SUB : (c + 1) * SUB, :], qu, NN)
                acc[1, wide, :] += dot(w_ref[sub, low * SUB : (c + 1) * SUB, :], gu, NN)
            yield
        span = slice(sub * SUB, sub * SUB + WIN)
        for out, left, right, factor in (
            (att_ref, 1, w_ref, 1.0),
            (dq_ref, 0, ds_ref, scale),
        ):
            product = dot(win_t[left, :, span], right[sub], NN)
            for side in range(2):
                at = pl.ds(pl.multiple_of(j * cols + (pair * 2 + side) * HEAD, HEAD), HEAD)
                tile = product[:, side * SUB : (side + 1) * SUB]
                out[rows, at] = (tile.T * factor).astype(jnp.bfloat16)
            yield

    def together(first, second, pattern):
        for letter in pattern:
            next(first if letter == "b" else second, None)

    pairs = GROUP // 2

    @pl.loop(0, KV_HEADS)
    def _(j):
        for which in range(2):
            own_copy(j, which).wait()
            load(j, which).wait()

    arrive(0)
    for _ in ahead(0, 0, 0):
        pass

    @pl.loop(0, KV_HEADS)
    def _(j):
        @pl.when(j + 1 < KV_HEADS)
        def _():
            each(lambda d, which: send(j + 1, d, which).start())

        for which in range(2):
            for r in range(0, W, SUB):
                win_t[which, :, r : r + SUB] = win[which, j, r : r + SUB, :].T
        acc[...] = jnp.zeros_like(acc)

        @pl.loop(0, pairs - 1)
        def _(pair):
            together(behind(j, pair, 0), ahead(j, pair, 1), PATTERN)
            together(behind(j, pair, 1), ahead(j, pair + 1, 0), PATTERN)

        together(behind(j, pairs - 1, 0), ahead(j, pairs - 1, 1), PATTERN)

        @pl.when(j + 1 < KV_HEADS)
        def _():
            arrive(j + 1)
            together(behind(j, pairs - 1, 1), ahead(j + 1, 0, 0), PATTERN)

        @pl.when(j + 1 == KV_HEADS)
        def _():
            for _ in behind(j, pairs - 1, 1):
                pass

        for which in range(2):
            factor = scale if which == 0 else 1.0
            out_part[which, j] = (acc[which, : W - T, :] * factor).astype(jnp.bfloat16)
            own[which, j] = acc[which, W - T :, :] * factor
        each(lambda d, which: back(j, d, which).start())

    @pl.loop(0, KV_HEADS)
    def _(j):
        each(lambda d, which: back(j, d, which).wait_recv())
        at = pl.ds(pl.multiple_of(j * HEAD, HEAD), HEAD)
        for which, ref in ((0, dk_ref), (1, dv_ref)):
            sums = own[which, j]
            for d in range(1, SPAN):
                sums = sums + in_part[which, j, d - 1].astype(jnp.float32)
            ref[:, at] = sums.astype(jnp.bfloat16)

    @pl.loop(0, KV_HEADS)
    def _(j):
        each(lambda d, which: send(j, d, which).wait_send())
        each(lambda d, which: back(j, d, which).wait_send())


def place_results(*refs):
    sem = refs[-1]
    copies = [pltpu.make_async_copy(refs[i], refs[4 + i], sem.at[i]) for i in range(4)]
    for copy in copies:
        copy.start()
    for copy in copies:
        copy.wait()


def local(queries, keys, values, out_grad, doc_lengths):
    T = queries.shape[0]
    W = SPAN * T
    WIN = W - SUB
    bf16, f32 = jnp.bfloat16, jnp.float32
    anywhere = pl.BlockSpec(memory_space=pl.ANY)
    vmem = pl.BlockSpec(memory_space=pltpu.VMEM)
    dma = pltpu.SemaphoreType.DMA
    parts = pl.pallas_call(
        kernel,
        out_shape=(
            jax.ShapeDtypeStruct(queries.shape, bf16),
            jax.ShapeDtypeStruct(queries.shape, bf16),
            jax.ShapeDtypeStruct(keys.shape, bf16),
            jax.ShapeDtypeStruct(keys.shape, bf16),
        ),
        in_specs=[anywhere] * 5,
        out_specs=(vmem, vmem, vmem, vmem),
        scratch_shapes=[
            pltpu.VMEM((KV_HEADS, T, GROUP * HEAD), bf16),
            pltpu.VMEM((KV_HEADS, T, GROUP * HEAD), bf16),
            pltpu.VMEM((2, KV_HEADS, W, HEAD), bf16),
            pltpu.VMEM((2, HEAD, W), bf16),
            pltpu.VMEM((T // SUB, WIN, SUB), f32),
            pltpu.VMEM((2, WIN, 2 * SUB), f32),
            pltpu.VMEM((2, WIN, 2 * SUB), f32),
            pltpu.VMEM((2, 3, WIN // SUB, 8, 2 * SUB), f32),
            pltpu.VMEM((2, WIN, 2 * SUB), bf16),
            pltpu.VMEM((2, WIN, 2 * SUB), bf16),
            pltpu.VMEM((2, W, HEAD), f32),
            pltpu.VMEM((2, KV_HEADS, T, HEAD), f32),
            pltpu.VMEM((2, KV_HEADS, W - T, HEAD), bf16),
            pltpu.VMEM((2, KV_HEADS, SPAN - 1, T, HEAD), bf16),
            pltpu.SMEM(doc_lengths.shape, jnp.int32),
            dma(()),
            dma((KV_HEADS, 2)),
            dma((KV_HEADS, 2)),
            dma((KV_HEADS, SPAN - 1, 2)),
            dma((KV_HEADS, SPAN - 1, 2)),
            dma((KV_HEADS, SPAN - 1, 2)),
            dma((KV_HEADS, SPAN - 1, 2)),
        ],
        compiler_params=pltpu.CompilerParams(
            collective_id=0, has_side_effects=True, vmem_limit_bytes=48 * 1024 * 1024
        ),
        name="attention",
    )(
        *(
            pltpu.with_memory_space_constraint(x, pltpu.HBM)
            for x in (queries, keys, values, out_grad, doc_lengths)
        )
    )
    return pl.pallas_call(
        place_results,
        out_shape=tuple(jax.ShapeDtypeStruct(x.shape, x.dtype) for x in parts),
        in_specs=[vmem] * 4,
        out_specs=(anywhere,) * 4,
        scratch_shapes=[dma((4,))],
        compiler_params=pltpu.CompilerParams(vmem_limit_bytes=1024 * 1024),
        name="results",
    )(*(pltpu.with_memory_space_constraint(x, pltpu.VMEM) for x in parts))


def solution(mesh):
    rows = P(("blk", "inner"), None)
    return jax.shard_map(
        local,
        mesh=mesh,
        in_specs=(rows, rows, rows, rows, P()),
        out_specs=(rows, rows, rows, rows),
        check_vma=False,
    )
```

```python
import math

import jax
import jax.numpy as jnp
from jax import lax
from jax.experimental import pallas as pl
from jax.experimental.pallas import tpu as pltpu
from jax.sharding import PartitionSpec as P

HEAD = 128
KV_HEADS = 4
GROUP = 8
SPAN = 4
RING = 4
SUB = 128
PATTERN = "bbabbabbababaaba"
AH = 4
BH = 7
MESH = pl.DeviceIdType.MESH
NT = (((1,), (1,)), ((), ()))
NN = (((1,), (0,)), ((), ()))


def dot(a, b, dims):
    return lax.dot_general(a, b, dims, preferred_element_type=jnp.float32)


def fold_rows(x, op):
    rows = x.shape[0]
    parts = [x[r : r + 8] for r in range(0, rows, 8)]
    while len(parts) > 1:
        parts = [op(parts[i], parts[i + 1]) for i in range(0, len(parts), 2)]
    return parts[0]


def kernel(
    q_hbm,
    k_hbm,
    v_hbm,
    g_hbm,
    len_hbm,
    att_ref,
    dq_ref,
    dk_ref,
    dv_ref,
    q_v,
    g_v,
    own_kv,
    win,
    win_t,
    bias,
    p_ref,
    dp_ref,
    stats,
    w_ref,
    ds_ref,
    acc,
    own,
    out_part,
    in_part,
    relay_out,
    relay_in,
    len_ref,
    load_sem,
    own_sem,
    len_sem,
    cross_send,
    cross_recv,
    share_send,
    share_recv,
    back_send,
    back_recv,
    relay_send,
    relay_recv,
):
    T = q_hbm.shape[0]
    W = SPAN * T
    WIN = W - SUB
    inner = lax.axis_size("inner")
    count = lax.axis_size("blk") * inner
    me = lax.axis_index("blk") * inner + lax.axis_index("inner")
    scale = 1.0 / math.sqrt(HEAD)
    cols = GROUP * HEAD

    def device(offset):
        there = lax.rem(me + offset + count, count)
        return (there // inner, lax.rem(there, inner))

    place = lax.rem(me, RING)

    def member(offset):
        there = me - place + lax.rem(place + offset + RING, RING)
        return (there // inner, lax.rem(there, inner))

    def load(j, which):
        src, dst = ((q_hbm, q_v), (g_hbm, g_v))[which]
        at = pl.ds(pl.multiple_of(j * cols, cols), cols)
        return pltpu.make_async_copy(src.at[:, at], dst.at[j], load_sem.at[j, which])

    def own_copy(which):
        return pltpu.make_async_copy((k_hbm, v_hbm)[which], own_kv.at[which], own_sem.at[which])

    def cross(j):
        return pltpu.make_async_remote_copy(
            src_ref=win.at[j, pl.ds(W - T, T), :],
            dst_ref=win.at[j, pl.ds(W, T), :],
            send_sem=cross_send.at[j],
            recv_sem=cross_recv.at[j],
            device_id=device(RING),
            device_id_type=MESH,
        )

    def share(j, m, relayed):
        return pltpu.make_async_remote_copy(
            src_ref=win.at[j, pl.ds(W if relayed else W - T, T), :],
            dst_ref=win.at[j, pl.ds((SPAN - 1 - m) * T, T), :],
            send_sem=share_send.at[j, m - 1],
            recv_sem=share_recv.at[j, m - 1],
            device_id=member(m),
            device_id_type=MESH,
        )

    def back(j, m, which):
        return pltpu.make_async_remote_copy(
            src_ref=out_part.at[which, j, pl.ds((SPAN - 1 - m) * T, T), :],
            dst_ref=in_part.at[which, j, m - 1],
            send_sem=back_send.at[j, m - 1, which],
            recv_sem=back_recv.at[j, m - 1, which],
            device_id=member(-m),
            device_id_type=MESH,
        )

    def cross_back(j, which):
        return pltpu.make_async_remote_copy(
            src_ref=relay_out.at[which, j],
            dst_ref=relay_in.at[which, j],
            send_sem=relay_send.at[j, which],
            recv_sem=relay_recv.at[j, which],
            device_id=device(-RING),
            device_id_type=MESH,
        )

    def each(fn):
        for m in range(1, SPAN):
            fn(m)

    def start_cross(j):
        cross(j).start()

    def start_shares(j):
        start_own(j)
        start_relayed(j)

    def start_own(j):
        for m in range(1, SPAN):

            @pl.when(place + m < RING)
            def _():
                share(j, m, False).start()

    def start_relayed(j):
        cross(j).wait_recv()
        for m in range(1, SPAN):

            @pl.when(place + m >= RING)
            def _():
                share(j, m, True).start()

    barrier = pltpu.get_barrier_semaphore()
    for m in range(1, RING):
        pl.semaphore_signal(barrier, inc=1, device_id=member(m), device_id_type=MESH)
    for sign in (1, -1):
        pl.semaphore_signal(barrier, inc=1, device_id=device(sign * RING), device_id_type=MESH)

    for which in range(2):
        own_copy(which).start()

    lengths = pltpu.make_async_copy(len_hbm, len_ref, len_sem)
    lengths.start()

    @pl.loop(0, KV_HEADS)
    def _(j):
        for which in range(2):
            load(j, which).start()

    for which in range(2):
        own_copy(which).wait()
        for j in range(KV_HEADS):
            win[j, W - T : W, which * HEAD : (which + 1) * HEAD] = own_kv[
                which, :, j * HEAD : (j + 1) * HEAD
            ]
    pl.semaphore_wait(barrier, RING + 1)

    start_cross(0)
    start_own(0)

    lengths.wait()

    q_pos = me * T + lax.broadcasted_iota(jnp.int32, (8, T), 1)

    def doc_step(i, carry):
        end, first = carry
        end = end + len_ref[i]
        return end, jnp.where(q_pos >= end, end, first)

    _, first = lax.fori_loop(
        0, len_ref.shape[0], doc_step, (jnp.int32(0), jnp.zeros((8, T), jnp.int32))
    )
    for sub in range(T // SUB):
        low = first[0:1, sub * SUB : (sub + 1) * SUB]
        high = q_pos[0:1, sub * SUB : (sub + 1) * SUB]
        start = (me - (SPAN - 1)) * T + sub * SUB
        for c in range(WIN // SUB):
            k_pos = start + c * SUB + lax.broadcasted_iota(jnp.int32, (SUB, SUB), 0)
            ok = (k_pos >= low) & (k_pos <= high)
            bias[sub, c * SUB : (c + 1) * SUB, :] = jnp.where(ok, 0.0, -1e30)

    def relay(j):
        for which in range(2):
            each(lambda m: back(j, m, which).wait_recv())
            mine = own[which, j]
            theirs = jnp.zeros((T, HEAD), jnp.float32)
            for m in range(1, SPAN):
                part = in_part[which, j, m - 1].astype(jnp.float32)
                keep = place + m < RING
                mine = mine + jnp.where(keep, part, 0.0)
                theirs = theirs + jnp.where(keep, 0.0, part)
            relay_out[which, j] = theirs.astype(jnp.bfloat16)
            cross_back(j, which).start()
            own[which, j] = mine

    def finish(j):
        at = pl.ds(pl.multiple_of(j * HEAD, HEAD), HEAD)
        for which, ref in ((0, dk_ref), (1, dv_ref)):
            cross_back(j, which).wait_recv()
            sums = own[which, j] + relay_in[which, j].astype(jnp.float32)
            ref[:, at] = sums.astype(jnp.bfloat16)

    start_relayed(0)
    start_cross(1)
    chunks = WIN // SUB
    to_exp2 = scale * math.log2(math.e)

    def arrive(j):
        each(lambda m: share(j, m, False).wait_recv())

    def stacked(ref, j, pair, sub):
        rows = slice(sub * SUB, (sub + 1) * SUB)
        parts = [
            ref[j, rows, pl.ds(pl.multiple_of((pair * 2 + side) * HEAD, HEAD), HEAD)]
            for side in range(2)
        ]
        return jnp.concatenate(parts, axis=0)

    def ahead(j, pair, sub):
        qu, gu = stacked(q_v, j, pair, sub), stacked(g_v, j, pair, sub)
        for c in range(chunks):
            at = slice(c * SUB, (c + 1) * SUB)
            keys = slice((sub + c) * SUB, (sub + c + 1) * SUB)
            extra = bias[sub, at, :]
            if c % AH == 0:
                wide = slice((sub + c) * SUB, (sub + min(c + AH, chunks)) * SUB)
                s_wide = dot(win[j, wide, :HEAD], qu, NT)
                dp_wide = dot(win[j, wide, HEAD:], gu, NT)
            part = slice(c % AH * SUB, (c % AH + 1) * SUB)
            s = s_wide[part] + jnp.concatenate([extra, extra], axis=1)
            dp = dp_wide[part]
            top = jnp.max(fold_rows(s, jnp.maximum), axis=0, keepdims=True)
            p = jnp.exp2((s - top) * to_exp2)
            p_ref[sub, at, :] = p
            dp_ref[sub, at, :] = dp
            stats[sub, 0, c] = jnp.broadcast_to(top, (8, 2 * SUB))
            stats[sub, 1, c] = fold_rows(p, jnp.add)
            stats[sub, 2, c] = fold_rows(p * dp, jnp.add)
            yield

    def behind(j, pair, sub, whole=True):
        qu, gu = stacked(q_v, j, pair, sub), stacked(g_v, j, pair, sub)
        rows = slice(sub * SUB, (sub + 1) * SUB)
        tops = [stats[sub, 0, c] for c in range(chunks)]
        top = tops[0]
        for c in range(1, chunks):
            top = jnp.maximum(top, tops[c])
        factors = [jnp.exp2((tops[c] - top) * to_exp2) for c in range(chunks)]
        total = sum(stats[sub, 1, c] * factors[c] for c in range(chunks))
        cross = sum(stats[sub, 2, c] * factors[c] for c in range(chunks))
        inv = 1.0 / jnp.sum(total, axis=0, keepdims=True)
        delta = jnp.sum(cross, axis=0, keepdims=True) * inv
        for c in range(chunks):
            at = slice(c * SUB, (c + 1) * SUB)
            keys = slice((sub + c) * SUB, (sub + c + 1) * SUB)
            w = p_ref[sub, at, :] * (factors[c][0:1] * inv)
            ds = (w * (dp_ref[sub, at, :] - delta)).astype(jnp.bfloat16)
            w = w.astype(jnp.bfloat16)
            w_ref[pair * 2 + sub, at, :] = w
            ds_ref[pair * 2 + sub, at, :] = ds
            if (c + 1) % BH == 0 or c + 1 == chunks:
                low = c // BH * BH
                wide = slice((sub + low) * SUB, (sub + c + 1) * SUB)
                acc[0, wide, :] += dot(ds_ref[pair * 2 + sub, low * SUB : (c + 1) * SUB, :], qu, NN)
                acc[1, wide, :] += dot(w_ref[pair * 2 + sub, low * SUB : (c + 1) * SUB, :], gu, NN)
            yield
        if whole:
            yield from products(j, pair, sub)

    def products(j, pair, sub):
        rows = slice(sub * SUB, (sub + 1) * SUB)
        span = slice(sub * SUB, sub * SUB + WIN)
        for out, left, right, factor in (
            (att_ref, 1, w_ref, 1.0),
            (dq_ref, 0, ds_ref, scale),
        ):
            product = dot(win_t[left, :, span], right[pair * 2 + sub], NN)
            for side in range(2):
                at = pl.ds(pl.multiple_of(j * cols + (pair * 2 + side) * HEAD, HEAD), HEAD)
                tile = product[:, side * SUB : (side + 1) * SUB]
                out[rows, at] = (tile.T * factor).astype(jnp.bfloat16)
            yield

    def together(first, second, pattern):
        for letter in pattern:
            next(first if letter == "b" else second, None)

    pairs = GROUP // 2

    @pl.loop(0, KV_HEADS)
    def _(j):
        for which in range(2):
            load(j, which).wait()

    arrive(0)
    for _ in ahead(0, 0, 0):
        pass

    def head(j, final):
        for which in range(2):
            for r in range(0, W, SUB):
                win_t[which, :, r : r + SUB] = win[
                    j, r : r + SUB, which * HEAD : (which + 1) * HEAD
                ].T
        acc[...] = jnp.zeros_like(acc)

        @pl.loop(0, pairs - 1)
        def _(pair):
            together(behind(j, pair, 0, not final), ahead(j, pair, 1), PATTERN)
            together(behind(j, pair, 1, not final), ahead(j, pair + 1, 0), PATTERN)

        if not final:

            @pl.when(j + 2 < KV_HEADS)
            def _():
                start_shares(j + 2)

            @pl.when(j + 3 < KV_HEADS)
            def _():
                start_cross(j + 3)

        together(behind(j, pairs - 1, 0, not final), ahead(j, pairs - 1, 1), PATTERN)
        if final:
            for _ in behind(j, pairs - 1, 1, False):
                pass
        else:
            arrive(j + 1)
            together(behind(j, pairs - 1, 1), ahead(j + 1, 0, 0), PATTERN)
        for which in range(2):
            factor = scale if which == 0 else 1.0
            out_part[which, j] = (acc[which, : W - T, :] * factor).astype(jnp.bfloat16)
            each(lambda m: back(j, m, which).start())
            own[which, j] = acc[which, W - T :, :] * factor

    @pl.loop(0, KV_HEADS - 1)
    def _(j):
        @pl.when(j == 0)
        def _():
            start_shares(1)
            start_cross(2)

        head(j, False)

        @pl.when(j > 0)
        def _():
            relay(j - 1)

    final = KV_HEADS - 1
    head(final, True)
    relay(final - 1)

    @pl.loop(0, pairs)
    def _(pair):
        for sub in range(2):
            for _ in products(final, pair, sub):
                pass

    @pl.loop(0, KV_HEADS - 1)
    def _(j):
        finish(j)

    relay(KV_HEADS - 1)
    finish(KV_HEADS - 1)

    @pl.loop(0, KV_HEADS)
    def _(j):
        each(lambda m: share(j, m, False).wait_send())
        cross(j).wait_send()
        for which in range(2):
            each(lambda m: back(j, m, which).wait_send())
            cross_back(j, which).wait_send()


def place_results(*refs):
    sem = refs[-1]
    copies = [pltpu.make_async_copy(refs[i], refs[4 + i], sem.at[i]) for i in range(4)]
    for copy in copies:
        copy.start()
    for copy in copies:
        copy.wait()


def local(queries, keys, values, out_grad, doc_lengths):
    T = queries.shape[0]
    W = SPAN * T
    WIN = W - SUB
    bf16, f32 = jnp.bfloat16, jnp.float32
    anywhere = pl.BlockSpec(memory_space=pl.ANY)
    vmem = pl.BlockSpec(memory_space=pltpu.VMEM)
    dma = pltpu.SemaphoreType.DMA
    parts = pl.pallas_call(
        kernel,
        out_shape=(
            jax.ShapeDtypeStruct(queries.shape, bf16),
            jax.ShapeDtypeStruct(queries.shape, bf16),
            jax.ShapeDtypeStruct(keys.shape, bf16),
            jax.ShapeDtypeStruct(keys.shape, bf16),
        ),
        in_specs=[anywhere] * 5,
        out_specs=(vmem, vmem, vmem, vmem),
        scratch_shapes=[
            pltpu.VMEM((KV_HEADS, T, GROUP * HEAD), bf16),
            pltpu.VMEM((KV_HEADS, T, GROUP * HEAD), bf16),
            pltpu.VMEM((2,) + keys.shape, bf16),
            pltpu.VMEM((KV_HEADS, W + T, 2 * HEAD), bf16),
            pltpu.VMEM((2, HEAD, W), bf16),
            pltpu.VMEM((T // SUB, WIN, SUB), f32),
            pltpu.VMEM((2, WIN, 2 * SUB), f32),
            pltpu.VMEM((2, WIN, 2 * SUB), f32),
            pltpu.VMEM((2, 3, WIN // SUB, 8, 2 * SUB), f32),
            pltpu.VMEM((GROUP, WIN, 2 * SUB), bf16),
            pltpu.VMEM((GROUP, WIN, 2 * SUB), bf16),
            pltpu.VMEM((2, W, HEAD), f32),
            pltpu.VMEM((2, KV_HEADS, T, HEAD), f32),
            pltpu.VMEM((2, KV_HEADS, W - T, HEAD), bf16),
            pltpu.VMEM((2, KV_HEADS, SPAN - 1, T, HEAD), bf16),
            pltpu.VMEM((2, KV_HEADS, T, HEAD), bf16),
            pltpu.VMEM((2, KV_HEADS, T, HEAD), bf16),
            pltpu.SMEM(doc_lengths.shape, jnp.int32),
            dma((KV_HEADS, 2)),
            dma((2,)),
            dma(()),
            dma((KV_HEADS,)),
            dma((KV_HEADS,)),
            dma((KV_HEADS, SPAN - 1)),
            dma((KV_HEADS, SPAN - 1)),
            dma((KV_HEADS, SPAN - 1, 2)),
            dma((KV_HEADS, SPAN - 1, 2)),
            dma((KV_HEADS, 2)),
            dma((KV_HEADS, 2)),
        ],
        compiler_params=pltpu.CompilerParams(
            collective_id=0, has_side_effects=True, vmem_limit_bytes=48 * 1024 * 1024
        ),
        name="attention",
    )(
        *(
            pltpu.with_memory_space_constraint(x, pltpu.HBM)
            for x in (queries, keys, values, out_grad, doc_lengths)
        )
    )
    return pl.pallas_call(
        place_results,
        out_shape=tuple(jax.ShapeDtypeStruct(x.shape, x.dtype) for x in parts),
        in_specs=[vmem] * 4,
        out_specs=(anywhere,) * 4,
        scratch_shapes=[dma((4,))],
        compiler_params=pltpu.CompilerParams(vmem_limit_bytes=1024 * 1024),
        name="results",
    )(*(pltpu.with_memory_space_constraint(x, pltpu.VMEM) for x in parts))


def solution(mesh):
    rows = P(("blk", "inner"), None)
    return jax.shard_map(
        local,
        mesh=mesh,
        in_specs=(rows, rows, rows, rows, P()),
        out_specs=(rows, rows, rows, rows),
        check_vma=False,
    )
```

```python
import math

import jax
import jax.numpy as jnp
from jax import lax
from jax.experimental import pallas as pl
from jax.experimental.pallas import tpu as pltpu
from jax.sharding import PartitionSpec as P

HEAD = 128
KV_HEADS = 4
GROUP = 8
SPAN = 4
RING = 4
SUB = 128
PATTERN = "bbabbabbababaaba"
AH = 4
BH = 7
MESH = pl.DeviceIdType.MESH
NT = (((1,), (1,)), ((), ()))
NN = (((1,), (0,)), ((), ()))


def dot(a, b, dims):
    return lax.dot_general(a, b, dims, preferred_element_type=jnp.float32)


def fold_rows(x, op):
    rows = x.shape[0]
    parts = [x[r : r + 8] for r in range(0, rows, 8)]
    while len(parts) > 1:
        parts = [op(parts[i], parts[i + 1]) for i in range(0, len(parts), 2)]
    return parts[0]


def kernel(
    q_hbm,
    k_hbm,
    v_hbm,
    g_hbm,
    len_hbm,
    att_ref,
    dq_ref,
    dk_ref,
    dv_ref,
    q_v,
    g_v,
    own_kv,
    win,
    win_t,
    bias,
    p_ref,
    dp_ref,
    stats,
    w_ref,
    ds_ref,
    acc,
    own,
    out_part,
    in_part,
    relay_out,
    relay_in,
    len_ref,
    load_sem,
    own_sem,
    len_sem,
    cross_send,
    cross_recv,
    share_send,
    share_recv,
    back_send,
    back_recv,
    relay_send,
    relay_recv,
):
    T = q_hbm.shape[0]
    W = SPAN * T
    WIN = W - SUB
    inner = lax.axis_size("inner")
    count = lax.axis_size("blk") * inner
    me = lax.axis_index("blk") * inner + lax.axis_index("inner")
    scale = 1.0 / math.sqrt(HEAD)
    cols = GROUP * HEAD

    def device(offset):
        there = lax.rem(me + offset + count, count)
        return (there // inner, lax.rem(there, inner))

    place = lax.rem(me, RING)

    def member(offset):
        there = me - place + lax.rem(place + offset + RING, RING)
        return (there // inner, lax.rem(there, inner))

    def load(j, which):
        src, dst = ((q_hbm, q_v), (g_hbm, g_v))[which]
        at = pl.ds(pl.multiple_of(j * cols, cols), cols)
        return pltpu.make_async_copy(src.at[:, at], dst.at[j], load_sem.at[j, which])

    def own_copy(which):
        return pltpu.make_async_copy((k_hbm, v_hbm)[which], own_kv.at[which], own_sem.at[which])

    def cross(j):
        return pltpu.make_async_remote_copy(
            src_ref=win.at[j, pl.ds(W - T, T), :],
            dst_ref=win.at[j, pl.ds(W, T), :],
            send_sem=cross_send.at[j],
            recv_sem=cross_recv.at[j],
            device_id=device(RING),
            device_id_type=MESH,
        )

    def share(j, m, relayed):
        return pltpu.make_async_remote_copy(
            src_ref=win.at[j, pl.ds(W if relayed else W - T, T), :],
            dst_ref=win.at[j, pl.ds((SPAN - 1 - m) * T, T), :],
            send_sem=share_send.at[j, m - 1],
            recv_sem=share_recv.at[j, m - 1],
            device_id=member(m),
            device_id_type=MESH,
        )

    def back(j, m, which):
        return pltpu.make_async_remote_copy(
            src_ref=out_part.at[which, j, pl.ds((SPAN - 1 - m) * T, T), :],
            dst_ref=in_part.at[which, j, m - 1],
            send_sem=back_send.at[j, m - 1, which],
            recv_sem=back_recv.at[j, m - 1, which],
            device_id=member(-m),
            device_id_type=MESH,
        )

    def cross_back(j, which):
        return pltpu.make_async_remote_copy(
            src_ref=relay_out.at[which, j],
            dst_ref=relay_in.at[which, j],
            send_sem=relay_send.at[j, which],
            recv_sem=relay_recv.at[j, which],
            device_id=device(-RING),
            device_id_type=MESH,
        )

    def each(fn):
        for m in range(1, SPAN):
            fn(m)

    def start_cross(j):
        cross(j).start()

    def start_shares(j):
        start_own(j)
        start_relayed(j)

    def start_own(j):
        for m in range(1, SPAN):

            @pl.when(place + m < RING)
            def _():
                share(j, m, False).start()

    def start_relayed(j):
        cross(j).wait_recv()
        for m in range(1, SPAN):

            @pl.when(place + m >= RING)
            def _():
                share(j, m, True).start()

    barrier = pltpu.get_barrier_semaphore()
    for m in range(1, RING):
        pl.semaphore_signal(barrier, inc=1, device_id=member(m), device_id_type=MESH)
    for sign in (1, -1):
        pl.semaphore_signal(barrier, inc=1, device_id=device(sign * RING), device_id_type=MESH)

    for which in range(2):
        own_copy(which).start()

    lengths = pltpu.make_async_copy(len_hbm, len_ref, len_sem)
    lengths.start()

    @pl.loop(0, KV_HEADS)
    def _(j):
        for which in range(2):
            load(j, which).start()

    for which in range(2):
        own_copy(which).wait()
        for j in range(KV_HEADS):
            win[j, W - T : W, which * HEAD : (which + 1) * HEAD] = own_kv[
                which, :, j * HEAD : (j + 1) * HEAD
            ]
    pl.semaphore_wait(barrier, RING + 1)

    start_cross(0)
    start_own(0)

    lengths.wait()

    q_pos = me * T + lax.broadcasted_iota(jnp.int32, (8, T), 1)

    def doc_step(i, carry):
        end, first = carry
        end = end + len_ref[i]
        return end, jnp.where(q_pos >= end, end, first)

    _, first = lax.fori_loop(
        0, len_ref.shape[0], doc_step, (jnp.int32(0), jnp.zeros((8, T), jnp.int32))
    )
    for sub in range(T // SUB):
        low = first[0:1, sub * SUB : (sub + 1) * SUB]
        high = q_pos[0:1, sub * SUB : (sub + 1) * SUB]
        start = (me - (SPAN - 1)) * T + sub * SUB
        for c in range(WIN // SUB):
            k_pos = start + c * SUB + lax.broadcasted_iota(jnp.int32, (SUB, SUB), 0)
            ok = (k_pos >= low) & (k_pos <= high)
            bias[sub, c * SUB : (c + 1) * SUB, :] = jnp.where(ok, 0.0, -1e30)

    def relay(j):
        for which in range(2):
            each(lambda m: back(j, m, which).wait_recv())
            mine = own[which, j]
            theirs = jnp.zeros((T, HEAD), jnp.float32)
            for m in range(1, SPAN):
                part = in_part[which, j, m - 1].astype(jnp.float32)
                keep = place + m < RING
                mine = mine + jnp.where(keep, part, 0.0)
                theirs = theirs + jnp.where(keep, 0.0, part)
            relay_out[which, j] = theirs.astype(jnp.bfloat16)
            cross_back(j, which).start()
            own[which, j] = mine

    def finish(j):
        at = pl.ds(pl.multiple_of(j * HEAD, HEAD), HEAD)
        for which, ref in ((0, dk_ref), (1, dv_ref)):
            cross_back(j, which).wait_recv()
            sums = own[which, j] + relay_in[which, j].astype(jnp.float32)
            ref[:, at] = sums.astype(jnp.bfloat16)

    start_relayed(0)
    start_cross(1)
    chunks = WIN // SUB
    to_exp2 = scale * math.log2(math.e)

    def arrive(j):
        each(lambda m: share(j, m, False).wait_recv())

    def stacked(ref, j, pair, sub):
        rows = slice(sub * SUB, (sub + 1) * SUB)
        parts = [
            ref[j, rows, pl.ds(pl.multiple_of((pair * 2 + side) * HEAD, HEAD), HEAD)]
            for side in range(2)
        ]
        return jnp.concatenate(parts, axis=0)

    def ahead(j, pair, sub):
        qu, gu = stacked(q_v, j, pair, sub), stacked(g_v, j, pair, sub)
        for c in range(chunks):
            at = slice(c * SUB, (c + 1) * SUB)
            keys = slice((sub + c) * SUB, (sub + c + 1) * SUB)
            extra = bias[sub, at, :]
            if c % AH == 0:
                wide = slice((sub + c) * SUB, (sub + min(c + AH, chunks)) * SUB)
                s_wide = dot(win[j, wide, :HEAD], qu, NT)
                dp_wide = dot(win[j, wide, HEAD:], gu, NT)
            part = slice(c % AH * SUB, (c % AH + 1) * SUB)
            s = s_wide[part] + jnp.concatenate([extra, extra], axis=1)
            dp = dp_wide[part]
            top = jnp.max(fold_rows(s, jnp.maximum), axis=0, keepdims=True)
            p = jnp.exp2((s - top) * to_exp2)
            p_ref[sub, at, :] = p
            dp_ref[sub, at, :] = dp
            stats[sub, 0, c] = jnp.broadcast_to(top, (8, 2 * SUB))
            stats[sub, 1, c] = fold_rows(p, jnp.add)
            stats[sub, 2, c] = fold_rows(p * dp, jnp.add)
            yield

    def behind(j, pair, sub, whole=True):
        qu, gu = stacked(q_v, j, pair, sub), stacked(g_v, j, pair, sub)
        rows = slice(sub * SUB, (sub + 1) * SUB)
        tops = [stats[sub, 0, c] for c in range(chunks)]
        top = tops[0]
        for c in range(1, chunks):
            top = jnp.maximum(top, tops[c])
        factors = [jnp.exp2((tops[c] - top) * to_exp2) for c in range(chunks)]
        total = sum(stats[sub, 1, c] * factors[c] for c in range(chunks))
        cross = sum(stats[sub, 2, c] * factors[c] for c in range(chunks))
        inv = 1.0 / jnp.sum(total, axis=0, keepdims=True)
        delta = jnp.sum(cross, axis=0, keepdims=True) * inv
        for c in range(chunks):
            at = slice(c * SUB, (c + 1) * SUB)
            keys = slice((sub + c) * SUB, (sub + c + 1) * SUB)
            w = p_ref[sub, at, :] * (factors[c][0:1] * inv)
            ds = (w * (dp_ref[sub, at, :] - delta)).astype(jnp.bfloat16)
            w = w.astype(jnp.bfloat16)
            w_ref[pair * 2 + sub, at, :] = w
            ds_ref[pair * 2 + sub, at, :] = ds
            if (c + 1) % BH == 0 or c + 1 == chunks:
                low = c // BH * BH
                wide = slice((sub + low) * SUB, (sub + c + 1) * SUB)
                acc[0, wide, :] += dot(ds_ref[pair * 2 + sub, low * SUB : (c + 1) * SUB, :], qu, NN)
                acc[1, wide, :] += dot(w_ref[pair * 2 + sub, low * SUB : (c + 1) * SUB, :], gu, NN)
            yield
        if whole:
            yield from products(j, pair, sub)

    def products(j, pair, sub):
        rows = slice(sub * SUB, (sub + 1) * SUB)
        span = slice(sub * SUB, sub * SUB + WIN)
        for out, left, right, factor in (
            (att_ref, 1, w_ref, 1.0),
            (dq_ref, 0, ds_ref, scale),
        ):
            product = dot(win_t[left, :, span], right[pair * 2 + sub], NN)
            for side in range(2):
                at = pl.ds(pl.multiple_of(j * cols + (pair * 2 + side) * HEAD, HEAD), HEAD)
                tile = product[:, side * SUB : (side + 1) * SUB]
                out[rows, at] = (tile.T * factor).astype(jnp.bfloat16)
            yield

    def together(first, second, pattern):
        for letter in pattern:
            next(first if letter == "b" else second, None)

    pairs = GROUP // 2

    @pl.loop(0, KV_HEADS)
    def _(j):
        for which in range(2):
            load(j, which).wait()

    arrive(0)
    for _ in ahead(0, 0, 0):
        pass

    def head(j, final):
        for which in range(2):
            for r in range(0, W, SUB):
                win_t[which, :, r : r + SUB] = win[
                    j, r : r + SUB, which * HEAD : (which + 1) * HEAD
                ].T
        acc[...] = jnp.zeros_like(acc)

        @pl.loop(0, pairs - 1)
        def _(pair):
            together(behind(j, pair, 0, not final), ahead(j, pair, 1), PATTERN)
            together(behind(j, pair, 1, not final), ahead(j, pair + 1, 0), PATTERN)

        if not final:

            @pl.when(j + 2 < KV_HEADS)
            def _():
                start_shares(j + 2)

            @pl.when(j + 3 < KV_HEADS)
            def _():
                start_cross(j + 3)

        together(behind(j, pairs - 1, 0, not final), ahead(j, pairs - 1, 1), PATTERN)
        if final:
            for _ in behind(j, pairs - 1, 1, False):
                pass
        else:
            arrive(j + 1)
            together(behind(j, pairs - 1, 1), ahead(j + 1, 0, 0), PATTERN)
        for which in range(2):
            factor = scale if which == 0 else 1.0
            out_part[which, j] = (acc[which, : W - T, :] * factor).astype(jnp.bfloat16)
            each(lambda m: back(j, m, which).start())
            own[which, j] = acc[which, W - T :, :] * factor

    @pl.loop(0, KV_HEADS - 1)
    def _(j):
        @pl.when(j == 0)
        def _():
            start_shares(1)
            start_cross(2)

        head(j, False)

        @pl.when(j > 1)
        def _():
            relay(j - 2)

    final = KV_HEADS - 1
    head(final, True)
    relay(final - 2)

    @pl.loop(0, pairs)
    def _(pair):
        for sub in range(2):
            for _ in products(final, pair, sub):
                pass

    relay(final - 1)
    relay(final)

    @pl.loop(0, KV_HEADS)
    def _(j):
        finish(j)

    @pl.loop(0, KV_HEADS)
    def _(j):
        each(lambda m: share(j, m, False).wait_send())
        cross(j).wait_send()
        for which in range(2):
            each(lambda m: back(j, m, which).wait_send())
            cross_back(j, which).wait_send()


def place_results(*refs):
    sem = refs[-1]
    copies = [pltpu.make_async_copy(refs[i], refs[4 + i], sem.at[i]) for i in range(4)]
    for copy in copies:
        copy.start()
    for copy in copies:
        copy.wait()


def local(queries, keys, values, out_grad, doc_lengths):
    T = queries.shape[0]
    W = SPAN * T
    WIN = W - SUB
    bf16, f32 = jnp.bfloat16, jnp.float32
    anywhere = pl.BlockSpec(memory_space=pl.ANY)
    vmem = pl.BlockSpec(memory_space=pltpu.VMEM)
    dma = pltpu.SemaphoreType.DMA
    parts = pl.pallas_call(
        kernel,
        out_shape=(
            jax.ShapeDtypeStruct(queries.shape, bf16),
            jax.ShapeDtypeStruct(queries.shape, bf16),
            jax.ShapeDtypeStruct(keys.shape, bf16),
            jax.ShapeDtypeStruct(keys.shape, bf16),
        ),
        in_specs=[anywhere] * 5,
        out_specs=(vmem, vmem, vmem, vmem),
        scratch_shapes=[
            pltpu.VMEM((KV_HEADS, T, GROUP * HEAD), bf16),
            pltpu.VMEM((KV_HEADS, T, GROUP * HEAD), bf16),
            pltpu.VMEM((2,) + keys.shape, bf16),
            pltpu.VMEM((KV_HEADS, W + T, 2 * HEAD), bf16),
            pltpu.VMEM((2, HEAD, W), bf16),
            pltpu.VMEM((T // SUB, WIN, SUB), f32),
            pltpu.VMEM((2, WIN, 2 * SUB), f32),
            pltpu.VMEM((2, WIN, 2 * SUB), f32),
            pltpu.VMEM((2, 3, WIN // SUB, 8, 2 * SUB), f32),
            pltpu.VMEM((GROUP, WIN, 2 * SUB), bf16),
            pltpu.VMEM((GROUP, WIN, 2 * SUB), bf16),
            pltpu.VMEM((2, W, HEAD), f32),
            pltpu.VMEM((2, KV_HEADS, T, HEAD), f32),
            pltpu.VMEM((2, KV_HEADS, W - T, HEAD), bf16),
            pltpu.VMEM((2, KV_HEADS, SPAN - 1, T, HEAD), bf16),
            pltpu.VMEM((2, KV_HEADS, T, HEAD), bf16),
            pltpu.VMEM((2, KV_HEADS, T, HEAD), bf16),
            pltpu.SMEM(doc_lengths.shape, jnp.int32),
            dma((KV_HEADS, 2)),
            dma((2,)),
            dma(()),
            dma((KV_HEADS,)),
            dma((KV_HEADS,)),
            dma((KV_HEADS, SPAN - 1)),
            dma((KV_HEADS, SPAN - 1)),
            dma((KV_HEADS, SPAN - 1, 2)),
            dma((KV_HEADS, SPAN - 1, 2)),
            dma((KV_HEADS, 2)),
            dma((KV_HEADS, 2)),
        ],
        compiler_params=pltpu.CompilerParams(
            collective_id=0, has_side_effects=True, vmem_limit_bytes=48 * 1024 * 1024
        ),
        name="attention",
    )(
        *(
            pltpu.with_memory_space_constraint(x, pltpu.HBM)
            for x in (queries, keys, values, out_grad, doc_lengths)
        )
    )
    return pl.pallas_call(
        place_results,
        out_shape=tuple(jax.ShapeDtypeStruct(x.shape, x.dtype) for x in parts),
        in_specs=[vmem] * 4,
        out_specs=(anywhere,) * 4,
        scratch_shapes=[dma((4,))],
        compiler_params=pltpu.CompilerParams(vmem_limit_bytes=1024 * 1024),
        name="results",
    )(*(pltpu.with_memory_space_constraint(x, pltpu.VMEM) for x in parts))


def solution(mesh):
    rows = P(("blk", "inner"), None)
    return jax.shard_map(
        local,
        mesh=mesh,
        in_specs=(rows, rows, rows, rows, P()),
        out_specs=(rows, rows, rows, rows),
        check_vma=False,
    )
```

```python
import math

import jax
import jax.numpy as jnp
from jax import lax
from jax.experimental import pallas as pl
from jax.experimental.pallas import tpu as pltpu
from jax.sharding import PartitionSpec as P

HEAD = 128
KV_HEADS = 4
GROUP = 8
SPAN = 4
RING = 4
SUB = 128
PATTERN = "bbabbabbababaaba"
AH = 4
BH = 7
MESH = pl.DeviceIdType.MESH
NT = (((1,), (1,)), ((), ()))
NN = (((1,), (0,)), ((), ()))


def dot(a, b, dims):
    return lax.dot_general(a, b, dims, preferred_element_type=jnp.float32)


def fold_rows(x, op):
    rows = x.shape[0]
    parts = [x[r : r + 8] for r in range(0, rows, 8)]
    while len(parts) > 1:
        parts = [op(parts[i], parts[i + 1]) for i in range(0, len(parts), 2)]
    return parts[0]


def kernel(
    q_hbm,
    k_hbm,
    v_hbm,
    g_hbm,
    len_hbm,
    att_ref,
    dq_ref,
    dk_ref,
    dv_ref,
    q_v,
    g_v,
    own_kv,
    win,
    win_t,
    bias,
    p_ref,
    dp_ref,
    stats,
    w_ref,
    ds_ref,
    acc,
    own,
    out_part,
    in_part,
    relay_out,
    relay_in,
    len_ref,
    load_sem,
    own_sem,
    len_sem,
    cross_send,
    cross_recv,
    share_send,
    share_recv,
    back_send,
    back_recv,
    relay_send,
    relay_recv,
):
    T = q_hbm.shape[0]
    W = SPAN * T
    WIN = W - SUB
    inner = lax.axis_size("inner")
    count = lax.axis_size("blk") * inner
    me = lax.axis_index("blk") * inner + lax.axis_index("inner")
    scale = 1.0 / math.sqrt(HEAD)
    cols = GROUP * HEAD

    def device(offset):
        there = lax.rem(me + offset + count, count)
        return (there // inner, lax.rem(there, inner))

    place = lax.rem(me, RING)

    def member(offset):
        there = me - place + lax.rem(place + offset + RING, RING)
        return (there // inner, lax.rem(there, inner))

    def load(j, which):
        src, dst = ((q_hbm, q_v), (g_hbm, g_v))[which]
        at = pl.ds(pl.multiple_of(j * cols, cols), cols)
        return pltpu.make_async_copy(src.at[:, at], dst.at[j], load_sem.at[j, which])

    def own_copy(which):
        return pltpu.make_async_copy((k_hbm, v_hbm)[which], own_kv.at[which], own_sem.at[which])

    def cross(j):
        return pltpu.make_async_remote_copy(
            src_ref=win.at[j, pl.ds(W - T, T), :],
            dst_ref=win.at[j, pl.ds(W, T), :],
            send_sem=cross_send.at[j],
            recv_sem=cross_recv.at[j],
            device_id=device(RING),
            device_id_type=MESH,
        )

    def share(j, m, relayed):
        return pltpu.make_async_remote_copy(
            src_ref=win.at[j, pl.ds(W if relayed else W - T, T), :],
            dst_ref=win.at[j, pl.ds((SPAN - 1 - m) * T, T), :],
            send_sem=share_send.at[j, m - 1],
            recv_sem=share_recv.at[j, m - 1],
            device_id=member(m),
            device_id_type=MESH,
        )

    def back(j, m, which):
        return pltpu.make_async_remote_copy(
            src_ref=out_part.at[which, j, pl.ds((SPAN - 1 - m) * T, T), :],
            dst_ref=in_part.at[which, j, m - 1],
            send_sem=back_send.at[j, m - 1, which],
            recv_sem=back_recv.at[j, m - 1, which],
            device_id=member(-m),
            device_id_type=MESH,
        )

    def cross_back(j, which):
        return pltpu.make_async_remote_copy(
            src_ref=relay_out.at[which, j],
            dst_ref=relay_in.at[which, j],
            send_sem=relay_send.at[j, which],
            recv_sem=relay_recv.at[j, which],
            device_id=device(-RING),
            device_id_type=MESH,
        )

    def each(fn):
        for m in range(1, SPAN):
            fn(m)

    def start_cross(j):
        cross(j).start()

    def start_shares(j):
        start_own(j)
        start_relayed(j)

    def start_own(j):
        for m in range(1, SPAN):

            @pl.when(place + m < RING)
            def _():
                share(j, m, False).start()

    def start_relayed(j):
        cross(j).wait_recv()
        for m in range(1, SPAN):

            @pl.when(place + m >= RING)
            def _():
                share(j, m, True).start()

    barrier = pltpu.get_barrier_semaphore()
    for m in range(1, RING):
        pl.semaphore_signal(barrier, inc=1, device_id=member(m), device_id_type=MESH)
    for sign in (1, -1):
        pl.semaphore_signal(barrier, inc=1, device_id=device(sign * RING), device_id_type=MESH)

    for which in range(2):
        own_copy(which).start()

    lengths = pltpu.make_async_copy(len_hbm, len_ref, len_sem)
    lengths.start()

    @pl.loop(0, KV_HEADS)
    def _(j):
        for which in range(2):
            load(j, which).start()

    for which in range(2):
        own_copy(which).wait()
        for j in range(KV_HEADS):
            win[j, W - T : W, which * HEAD : (which + 1) * HEAD] = own_kv[
                which, :, j * HEAD : (j + 1) * HEAD
            ]
    pl.semaphore_wait(barrier, RING + 1)

    start_cross(0)
    start_own(0)

    lengths.wait()

    q_pos = me * T + lax.broadcasted_iota(jnp.int32, (8, T), 1)

    def doc_step(i, carry):
        end, first = carry
        end = end + len_ref[i]
        return end, jnp.where(q_pos >= end, end, first)

    _, first = lax.fori_loop(
        0, len_ref.shape[0], doc_step, (jnp.int32(0), jnp.zeros((8, T), jnp.int32))
    )
    for sub in range(T // SUB):
        low = first[0:1, sub * SUB : (sub + 1) * SUB]
        high = q_pos[0:1, sub * SUB : (sub + 1) * SUB]
        start = (me - (SPAN - 1)) * T + sub * SUB
        for c in range(WIN // SUB):
            k_pos = start + c * SUB + lax.broadcasted_iota(jnp.int32, (SUB, SUB), 0)
            ok = (k_pos >= low) & (k_pos <= high)
            bias[sub, c * SUB : (c + 1) * SUB, :] = jnp.where(ok, 0.0, -1e30)

    def relay(j):
        for which in range(2):
            each(lambda m: back(j, m, which).wait_recv())
            mine = own[which, j]
            theirs = jnp.zeros((T, HEAD), jnp.float32)
            for m in range(1, SPAN):
                part = in_part[which, j, m - 1].astype(jnp.float32)
                keep = place + m < RING
                mine = mine + jnp.where(keep, part, 0.0)
                theirs = theirs + jnp.where(keep, 0.0, part)
            relay_out[which, j] = theirs.astype(jnp.bfloat16)
            cross_back(j, which).start()
            own[which, j] = mine

    def finish(j):
        at = pl.ds(pl.multiple_of(j * HEAD, HEAD), HEAD)
        for which, ref in ((0, dk_ref), (1, dv_ref)):
            cross_back(j, which).wait_recv()
            sums = own[which, j] + relay_in[which, j].astype(jnp.float32)
            ref[:, at] = sums.astype(jnp.bfloat16)

    start_relayed(0)
    start_cross(1)
    start_cross(2)
    chunks = WIN // SUB
    to_exp2 = scale * math.log2(math.e)

    def arrive(j):
        each(lambda m: share(j, m, False).wait_recv())

    def stacked(ref, j, pair, sub):
        rows = slice(sub * SUB, (sub + 1) * SUB)
        parts = [
            ref[j, rows, pl.ds(pl.multiple_of((pair * 2 + side) * HEAD, HEAD), HEAD)]
            for side in range(2)
        ]
        return jnp.concatenate(parts, axis=0)

    def ahead(j, pair, sub):
        qu, gu = stacked(q_v, j, pair, sub), stacked(g_v, j, pair, sub)
        for c in range(chunks):
            at = slice(c * SUB, (c + 1) * SUB)
            keys = slice((sub + c) * SUB, (sub + c + 1) * SUB)
            extra = bias[sub, at, :]
            if c % AH == 0:
                wide = slice((sub + c) * SUB, (sub + min(c + AH, chunks)) * SUB)
                s_wide = dot(win[j, wide, :HEAD], qu, NT)
                dp_wide = dot(win[j, wide, HEAD:], gu, NT)
            part = slice(c % AH * SUB, (c % AH + 1) * SUB)
            s = s_wide[part] + jnp.concatenate([extra, extra], axis=1)
            dp = dp_wide[part]
            top = jnp.max(fold_rows(s, jnp.maximum), axis=0, keepdims=True)
            p = jnp.exp2((s - top) * to_exp2)
            p_ref[sub, at, :] = p
            dp_ref[sub, at, :] = dp
            stats[sub, 0, c] = jnp.broadcast_to(top, (8, 2 * SUB))
            stats[sub, 1, c] = fold_rows(p, jnp.add)
            stats[sub, 2, c] = fold_rows(p * dp, jnp.add)
            yield

    def behind(j, pair, sub, whole=True):
        qu, gu = stacked(q_v, j, pair, sub), stacked(g_v, j, pair, sub)
        rows = slice(sub * SUB, (sub + 1) * SUB)
        tops = [stats[sub, 0, c] for c in range(chunks)]
        top = tops[0]
        for c in range(1, chunks):
            top = jnp.maximum(top, tops[c])
        factors = [jnp.exp2((tops[c] - top) * to_exp2) for c in range(chunks)]
        total = sum(stats[sub, 1, c] * factors[c] for c in range(chunks))
        cross = sum(stats[sub, 2, c] * factors[c] for c in range(chunks))
        inv = 1.0 / jnp.sum(total, axis=0, keepdims=True)
        delta = jnp.sum(cross, axis=0, keepdims=True) * inv
        for c in range(chunks):
            at = slice(c * SUB, (c + 1) * SUB)
            keys = slice((sub + c) * SUB, (sub + c + 1) * SUB)
            w = p_ref[sub, at, :] * (factors[c][0:1] * inv)
            ds = (w * (dp_ref[sub, at, :] - delta)).astype(jnp.bfloat16)
            w = w.astype(jnp.bfloat16)
            w_ref[pair * 2 + sub, at, :] = w
            ds_ref[pair * 2 + sub, at, :] = ds
            if (c + 1) % BH == 0 or c + 1 == chunks:
                low = c // BH * BH
                wide = slice((sub + low) * SUB, (sub + c + 1) * SUB)
                acc[0, wide, :] += dot(ds_ref[pair * 2 + sub, low * SUB : (c + 1) * SUB, :], qu, NN)
                acc[1, wide, :] += dot(w_ref[pair * 2 + sub, low * SUB : (c + 1) * SUB, :], gu, NN)
            yield
        if whole:
            yield from products(j, pair, sub)

    def products(j, pair, sub):
        rows = slice(sub * SUB, (sub + 1) * SUB)
        span = slice(sub * SUB, sub * SUB + WIN)
        for out, left, right, factor in (
            (att_ref, 1, w_ref, 1.0),
            (dq_ref, 0, ds_ref, scale),
        ):
            product = dot(win_t[left, :, span], right[pair * 2 + sub], NN)
            for side in range(2):
                at = pl.ds(pl.multiple_of(j * cols + (pair * 2 + side) * HEAD, HEAD), HEAD)
                tile = product[:, side * SUB : (side + 1) * SUB]
                out[rows, at] = (tile.T * factor).astype(jnp.bfloat16)
            yield

    def together(first, second, pattern):
        for letter in pattern:
            next(first if letter == "b" else second, None)

    pairs = GROUP // 2

    @pl.loop(0, KV_HEADS)
    def _(j):
        for which in range(2):
            load(j, which).wait()

    arrive(0)
    for _ in ahead(0, 0, 0):
        pass

    def head(j, final):
        for which in range(2):
            for r in range(0, W, SUB):
                win_t[which, :, r : r + SUB] = win[
                    j, r : r + SUB, which * HEAD : (which + 1) * HEAD
                ].T
        acc[...] = jnp.zeros_like(acc)

        @pl.loop(0, pairs - 1)
        def _(pair):
            together(behind(j, pair, 0, not final), ahead(j, pair, 1), PATTERN)
            together(behind(j, pair, 1, not final), ahead(j, pair + 1, 0), PATTERN)

        if not final:

            @pl.when(j + 2 < KV_HEADS)
            def _():
                start_shares(j + 2)

        together(behind(j, pairs - 1, 0, not final), ahead(j, pairs - 1, 1), PATTERN)
        if final:
            for _ in behind(j, pairs - 1, 1, False):
                pass
        else:
            arrive(j + 1)
            together(behind(j, pairs - 1, 1), ahead(j + 1, 0, 0), PATTERN)
        for which in range(2):
            factor = scale if which == 0 else 1.0
            out_part[which, j] = (acc[which, : W - T, :] * factor).astype(jnp.bfloat16)
            each(lambda m: back(j, m, which).start())
            own[which, j] = acc[which, W - T :, :] * factor

    @pl.loop(0, KV_HEADS - 1)
    def _(j):
        @pl.when(j == 0)
        def _():
            start_shares(1)
            start_cross(3)

        head(j, False)

        @pl.when(j > 1)
        def _():
            relay(j - 2)

    final = KV_HEADS - 1
    head(final, True)
    relay(final - 2)

    @pl.loop(0, pairs)
    def _(pair):
        for sub in range(2):
            for _ in products(final, pair, sub):
                pass

    relay(final - 1)
    relay(final)

    @pl.loop(0, KV_HEADS)
    def _(j):
        finish(j)

    @pl.loop(0, KV_HEADS)
    def _(j):
        each(lambda m: share(j, m, False).wait_send())
        cross(j).wait_send()
        for which in range(2):
            each(lambda m: back(j, m, which).wait_send())
            cross_back(j, which).wait_send()


def place_results(*refs):
    sem = refs[-1]
    copies = [pltpu.make_async_copy(refs[i], refs[4 + i], sem.at[i]) for i in range(4)]
    for copy in copies:
        copy.start()
    for copy in copies:
        copy.wait()


def local(queries, keys, values, out_grad, doc_lengths):
    T = queries.shape[0]
    W = SPAN * T
    WIN = W - SUB
    bf16, f32 = jnp.bfloat16, jnp.float32
    anywhere = pl.BlockSpec(memory_space=pl.ANY)
    vmem = pl.BlockSpec(memory_space=pltpu.VMEM)
    dma = pltpu.SemaphoreType.DMA
    parts = pl.pallas_call(
        kernel,
        out_shape=(
            jax.ShapeDtypeStruct(queries.shape, bf16),
            jax.ShapeDtypeStruct(queries.shape, bf16),
            jax.ShapeDtypeStruct(keys.shape, bf16),
            jax.ShapeDtypeStruct(keys.shape, bf16),
        ),
        in_specs=[anywhere] * 5,
        out_specs=(vmem, vmem, vmem, vmem),
        scratch_shapes=[
            pltpu.VMEM((KV_HEADS, T, GROUP * HEAD), bf16),
            pltpu.VMEM((KV_HEADS, T, GROUP * HEAD), bf16),
            pltpu.VMEM((2,) + keys.shape, bf16),
            pltpu.VMEM((KV_HEADS, W + T, 2 * HEAD), bf16),
            pltpu.VMEM((2, HEAD, W), bf16),
            pltpu.VMEM((T // SUB, WIN, SUB), f32),
            pltpu.VMEM((2, WIN, 2 * SUB), f32),
            pltpu.VMEM((2, WIN, 2 * SUB), f32),
            pltpu.VMEM((2, 3, WIN // SUB, 8, 2 * SUB), f32),
            pltpu.VMEM((GROUP, WIN, 2 * SUB), bf16),
            pltpu.VMEM((GROUP, WIN, 2 * SUB), bf16),
            pltpu.VMEM((2, W, HEAD), f32),
            pltpu.VMEM((2, KV_HEADS, T, HEAD), f32),
            pltpu.VMEM((2, KV_HEADS, W - T, HEAD), bf16),
            pltpu.VMEM((2, KV_HEADS, SPAN - 1, T, HEAD), bf16),
            pltpu.VMEM((2, KV_HEADS, T, HEAD), bf16),
            pltpu.VMEM((2, KV_HEADS, T, HEAD), bf16),
            pltpu.SMEM(doc_lengths.shape, jnp.int32),
            dma((KV_HEADS, 2)),
            dma((2,)),
            dma(()),
            dma((KV_HEADS,)),
            dma((KV_HEADS,)),
            dma((KV_HEADS, SPAN - 1)),
            dma((KV_HEADS, SPAN - 1)),
            dma((KV_HEADS, SPAN - 1, 2)),
            dma((KV_HEADS, SPAN - 1, 2)),
            dma((KV_HEADS, 2)),
            dma((KV_HEADS, 2)),
        ],
        compiler_params=pltpu.CompilerParams(
            collective_id=0, has_side_effects=True, vmem_limit_bytes=48 * 1024 * 1024
        ),
        name="attention",
    )(
        *(
            pltpu.with_memory_space_constraint(x, pltpu.HBM)
            for x in (queries, keys, values, out_grad, doc_lengths)
        )
    )
    return pl.pallas_call(
        place_results,
        out_shape=tuple(jax.ShapeDtypeStruct(x.shape, x.dtype) for x in parts),
        in_specs=[vmem] * 4,
        out_specs=(anywhere,) * 4,
        scratch_shapes=[dma((4,))],
        compiler_params=pltpu.CompilerParams(vmem_limit_bytes=1024 * 1024),
        name="results",
    )(*(pltpu.with_memory_space_constraint(x, pltpu.VMEM) for x in parts))


def solution(mesh):
    rows = P(("blk", "inner"), None)
    return jax.shard_map(
        local,
        mesh=mesh,
        in_specs=(rows, rows, rows, rows, P()),
        out_specs=(rows, rows, rows, rows),
        check_vma=False,
    )
```
